32 devices in a mesh: ctx: 16 (over z, y, x), head: 2 (over core).
Axes of the slice: x: 2, y: 2, z: 4, core: 2. Of those that a mesh axis runs over, the one named last changes fastest.
Arguments:
- queries: bfloat16 [4096, 16, 128], P('ctx', 'head'), may hold values from -6 to 6
- key_vecs: bfloat16 [4096, 16, 128], P('ctx', 'head'), may hold values from -16 to 16
- values: bfloat16 [4096, 16, 128], P('ctx', 'head'), may hold values from -6 to 6
- log_decay: float32 [16, 4096], P('head', 'ctx'), may hold values from -1.5 to 0
- ridge_diag: float32 [16, 128], P('head'), may hold values from 0.05 to 1
- residual: bfloat16 [4096, 2048], P(('ctx', 'head')), may hold values from -6 to 6
- w_out: bfloat16 [2048, 2048], P('head'), may hold values from -0.125 to 0.125
- norm_gain: float32 [2048], replicated, may hold values from 0.1 to 1.9
- routes: int32 [4096, 8], P(('ctx', 'head')), may hold values from 0 to 31, as said below
- gate_probs: float32 [4096, 8], P(('ctx', 'head')), may hold values from 0.1 to 0.5
- w_gate: bfloat16 [32, 2048, 768], P(('ctx', 'head')), may hold values from -0.125 to 0.125
- w_up: bfloat16 [32, 2048, 768], P(('ctx', 'head')), may hold values from -0.125 to 0.125
- w_down: bfloat16 [32, 768, 2048], P(('ctx', 'head')), may hold values from -0.21875 to 0.21875
Outputs:
- attended: bfloat16 [4096, 2048], P(('ctx', 'head'))
- layer_out: bfloat16 [4096, 2048], P(('ctx', 'head'))
The draws below stay inside these ranges and needn't reach their ends.
Inputs may be any that keep to these rules, and one draw needn't show every extreme that they name: `routes`: the k-th route of every token names an expert of group k, the experts k * 4 to (k + 1) * 4 - 1. In every aligned block of 128 tokens (the tokens of one device) no expert is named more than 64 times, and in every group one expert is named exactly 64 times in every block.
All inputs are finite; a program needn't handle non-finite values.
Results may differ from the reference program's by a relative error of at most 0.012.
Values may be sent and summed in bfloat16 or wider, within the bound.
No kernel may reach another device: no remote copies, remote signals or barrier semaphores. Data moves between devices by JAX's collectives and lax.ppermute only.
A program may use at most 192 MiB of HBM per device.

```python
import math
import jax
import jax.numpy as jnp
from jax import lax

D = 2048
HEADS = 16
HD = 128
FFE = 768
TOPK = 8
CG_STEPS = 4
TOK_DEV = 256
WINDOW_TOKENS = 4096
EXPERTS = 32
MOE_DEV = 128
CAP = 64


def draw_key_vecs(key, part):
    normal_part = jax.random.normal(jax.random.fold_in(key, 11), (WINDOW_TOKENS, HEADS, HD), jnp.float32)
    chan_scale = jnp.exp(jax.random.uniform(jax.random.fold_in(key, 12), (HEADS, HD), jnp.float32, math.log(0.3), math.log(3.0)))
    mixing = jnp.eye(HD, dtype=jnp.float32)[None] + 0.6 * jax.random.normal(jax.random.fold_in(key, 13), (HEADS, HD, HD), jnp.float32) / math.sqrt(HD)
    shaped = jnp.einsum('thd,hde->the', normal_part * chan_scale[None], mixing)
    return jnp.clip(shaped, -16.0, 16.0).astype(jnp.bfloat16)


def draw_log_decay(key, part):
    segments = WINDOW_TOKENS // TOK_DEV
    slow_share = 0.5
    slow_mask = jax.random.uniform(jax.random.fold_in(key, 31), (HEADS,), jnp.float32) < slow_share
    slow_rate = jax.random.uniform(jax.random.fold_in(key, 32), (HEADS,), jnp.float32, 0.15, 0.45) * math.log(10.0) / WINDOW_TOKENS
    fast_rate = math.log(10.0) / jax.random.uniform(jax.random.fold_in(key, 33), (HEADS,), jnp.float32, 30.0, 50.0)
    rate_head = jnp.where(slow_mask, slow_rate, fast_rate)
    seg_factor = jnp.exp(jax.random.uniform(jax.random.fold_in(key, 34), (HEADS, segments), jnp.float32, math.log(0.5), math.log(2.0)))
    tok_factor = jnp.exp(jax.random.uniform(jax.random.fold_in(key, 35), (HEADS, WINDOW_TOKENS), jnp.float32, math.log(0.7), math.log(1.4)))
    decayed_state = -rate_head[:, None] * jnp.repeat(seg_factor, TOK_DEV, axis=1) * tok_factor
    segment_position = jax.random.randint(jax.random.fold_in(key, 36), (2,), 0, WINDOW_TOKENS)
    segment_keep_factor = jax.random.uniform(jax.random.fold_in(key, 37), (2,), jnp.float32, 0.6, 0.8)
    token_position = jnp.arange(WINDOW_TOKENS)
    segment_log_decay = jnp.sum(jnp.where(token_position[None, :] == segment_position[:, None], jnp.log(segment_keep_factor)[:, None], 0.0), axis=0)
    return (decayed_state + segment_log_decay[None, :]).astype(jnp.float32)


def draw_routes(key, part):
    block_count = WINDOW_TOKENS // MOE_DEV
    group_size = EXPERTS // TOPK
    free_span = MOE_DEV - CAP
    hot_pick = jax.random.randint(jax.random.fold_in(key, 21), (TOPK,), 0, group_size)
    col_total = block_count * TOPK
    col_index = jnp.arange(col_total)
    rank_key = jax.random.fold_in(key, 22)
    other_key = jax.random.fold_in(key, 23)
    row_ranks = jax.vmap(lambda col_id: jax.random.permutation(jax.random.fold_in(rank_key, col_id), MOE_DEV))(col_index)
    row_ranks = row_ranks.reshape(block_count, TOPK, MOE_DEV)
    other_perm = jax.vmap(lambda col_id: jax.random.permutation(jax.random.fold_in(other_key, col_id), group_size - 1))(col_index)
    other_perm = other_perm.reshape(block_count, TOPK, group_size - 1)
    beyond = jnp.maximum(row_ranks - CAP, 0)
    tier_level = jnp.where(row_ranks < CAP, 0, 1 + (group_size - 1) * beyond * (free_span + beyond) // (2 * free_span * free_span))
    picked = jnp.take_along_axis(other_perm, jnp.maximum(tier_level - 1, 0), axis=2)
    local_id = jnp.where(tier_level == 0, hot_pick[None, :, None], (hot_pick[None, :, None] + 1 + picked) % group_size)
    expert = local_id + (jnp.arange(TOPK) * group_size)[None, :, None]
    return expert.transpose(0, 2, 1).reshape(WINDOW_TOKENS, TOPK).astype(jnp.int32)


def block_scale(key, extent, cuts, least, largest):
    factor_of, own = 1.0, jax.random.fold_in(key, 6)
    for axis_at, shards_of in cuts:
        draws = jnp.exp(jax.random.uniform(jax.random.fold_in(own, axis_at), (shards_of,), jnp.float32, least / len(cuts), largest / len(cuts)))
        factor_of = factor_of * jnp.repeat(draws, extent[axis_at] // shards_of).reshape([-1 if axis == axis_at else 1 for axis in range(len(extent))])
    return factor_of


def bell_draw(stream_key, dims, deviation, reach, split=(), kind=jnp.bfloat16):
    entries = jax.random.normal(stream_key, dims, jnp.float32) * deviation
    if len(split) > 0:
        entries = block_scale(stream_key, dims, split, -0.22, 0.18) * entries
    return jnp.clip(entries, min=-reach, max=reach).astype(kind)


def setup_inputs(seed: int = 0) -> dict:
    keys = jax.random.split(jax.random.key(seed), 14)
    return {
        "queries": bell_draw(keys[0], (WINDOW_TOKENS, HEADS, HD), 1.0, 6.0, ((0, 16), (1, 2))),
        "key_vecs": draw_key_vecs(jax.random.fold_in(keys[13], 71), 0),
        "values": bell_draw(keys[2], (WINDOW_TOKENS, HEADS, HD), 1.0, 6.0, ((0, 16), (1, 2))),
        "log_decay": draw_log_decay(jax.random.fold_in(keys[13], 71), 0),
        "ridge_diag": jnp.clip(jnp.exp(math.log(1.0) - 2.9957323 * jax.random.uniform(keys[4], (HEADS, HD), jnp.float32) ** block_scale(keys[4], (HEADS, HD), ((0, 2),), -0.2, 0.2)), 0.05, 1.0),
        "residual": bell_draw(keys[5], (WINDOW_TOKENS, D), 1.0, 6.0, ((0, 32),)),
        "w_out": bell_draw(keys[6], (HEADS * HD, D), (HEADS * HD) ** -0.5, 0.125, ((0, 2),)),
        "norm_gain": jnp.clip(1.0 + 0.18 * jax.random.normal(keys[7], (D,), jnp.float32), 0.1, 1.9),
        "routes": draw_routes(jax.random.fold_in(keys[13], 71), 0),
        "gate_probs": jnp.clip(0.1 + 0.4 * jax.random.uniform(keys[9], (WINDOW_TOKENS, TOPK), jnp.float32) ** block_scale(keys[9], (WINDOW_TOKENS, TOPK), ((0, 32),), -0.2, 0.2), 0.1, 0.5),
        "w_gate": bell_draw(keys[10], (EXPERTS, D, FFE), D ** -0.5, 0.125, ((0, 32),)),
        "w_up": bell_draw(keys[11], (EXPERTS, D, FFE), D ** -0.5, 0.125, ((0, 32),)),
        "w_down": bell_draw(keys[12], (EXPERTS, FFE, D), FFE ** -0.5, 0.21875, ((0, 32),)),
    }


exact_prec = lax.Precision.HIGHEST
norm_eps = 1e-06

def unit_rows(vectors):
    floats = vectors.astype(jnp.float32)
    return floats * lax.rsqrt(lax.optimization_barrier(jnp.sum(floats * floats, axis=-1, keepdims=True)) + norm_eps)

def rounded_keys(key_vecs):
    narrow = lax.optimization_barrier(unit_rows(key_vecs).astype(jnp.bfloat16))
    return narrow.astype(jnp.float32)

def causal_weights(cumul_log):
    length = cumul_log.shape[1]
    lower_mask = jnp.arange(length)[:, None] >= jnp.arange(length)[None, :]
    gap_log = cumul_log[:, :, None] - cumul_log[:, None, :]
    return jnp.where(lower_mask[None], jnp.exp(jnp.where(lower_mask[None], gap_log, 0.0)), 0.0)

def apply_system(probe_vec, gram_prior, start_w, weights, key_f, ridge_diag):
    prior_part = start_w[:, :, None] * jnp.einsum('hte,hde->htd', probe_vec, gram_prior, precision=exact_prec)
    scores = jnp.einsum('htd,hsd->hts', probe_vec, key_f, precision=exact_prec) * weights
    inner_part = jnp.einsum('hts,hsd->htd', scores, key_f, precision=exact_prec)
    return prior_part + inner_part + ridge_diag[:, None, :] * probe_vec

def conj_grad(rhs_vec, gram_prior, start_w, weights, key_f, ridge_diag):
    answer = jnp.zeros_like(rhs_vec)
    remain = rhs_vec
    direction = rhs_vec
    norm_now = lax.optimization_barrier(jnp.sum(remain * remain, axis=-1))
    for step_id in range(CG_STEPS):
        applied = apply_system(direction, gram_prior, start_w, weights, key_f, ridge_diag)
        step_len = norm_now / lax.optimization_barrier(jnp.sum(direction * applied, axis=-1))
        answer = answer + step_len[:, :, None] * direction
        remain = remain - step_len[:, :, None] * applied
        norm_next = lax.optimization_barrier(jnp.sum(remain * remain, axis=-1))
        direction = remain + (norm_next / norm_now)[:, :, None] * direction
        norm_now = norm_next
    return answer

def read_out(answer, value_prior, start_w, weights, key_f, value_f):
    prior_part = start_w[:, :, None] * jnp.einsum('htd,hed->hte', answer, value_prior, precision=exact_prec)
    scores = jnp.einsum('htd,hsd->hts', answer, key_f, precision=exact_prec) * weights
    return prior_part + jnp.einsum('hts,hse->hte', scores, value_f, precision=exact_prec)

def block_states(key_f, value_f, cumul_log):
    end_w = jnp.exp(cumul_log[:, -1:] - cumul_log)[:, :, None]
    gram_loc = jnp.einsum('hsd,hse->hde', key_f * end_w, key_f, precision=exact_prec)
    value_loc = jnp.einsum('hse,hsd->hed', value_f * end_w, key_f, precision=exact_prec)
    return (cumul_log[:, -1], gram_loc, value_loc)

def reference(queries, key_vecs, values, log_decay, ridge_diag, residual, w_out, norm_gain, routes, gate_probs, w_gate, w_up, w_down):
    heads_all = queries.shape[1]
    head_dim = queries.shape[2]
    block_count = WINDOW_TOKENS // TOK_DEV

    def to_blocks(array):
        return array.reshape(block_count, TOK_DEV, heads_all, head_dim).transpose(0, 2, 1, 3)
    q_blocks = to_blocks(unit_rows(queries))
    k_blocks = to_blocks(rounded_keys(key_vecs))
    v_blocks = to_blocks(values.astype(jnp.float32))
    d_blocks = log_decay.reshape(heads_all, block_count, TOK_DEV).transpose(1, 0, 2)

    def stretch_step(state_pair, inputs):
        gram_prior, value_prior = state_pair
        query_unit, key_f, value_f, decay_blk = inputs
        cumul_log = jnp.cumsum(decay_blk, axis=1)
        start_w = jnp.exp(cumul_log)
        weights = causal_weights(cumul_log)
        answer = conj_grad(query_unit, gram_prior, start_w, weights, key_f, ridge_diag)
        mesa_out = read_out(answer, value_prior, start_w, weights, key_f, value_f)
        tail_log, gram_loc, value_loc = block_states(key_f, value_f, cumul_log)
        factor = jnp.exp(tail_log)[:, None, None]
        return ((factor * gram_prior + gram_loc, factor * value_prior + value_loc), mesa_out)
    zero_state = jnp.zeros((heads_all, head_dim, head_dim), jnp.float32)
    final_state, mesa_all = lax.scan(stretch_step, (zero_state, zero_state), (q_blocks, k_blocks, v_blocks, d_blocks))
    mesa_rows = mesa_all.transpose(0, 2, 1, 3).reshape(WINDOW_TOKENS, heads_all * head_dim).astype(jnp.bfloat16)
    attended = (residual.astype(jnp.float32) + jnp.dot(mesa_rows, w_out, preferred_element_type=jnp.float32)).astype(jnp.bfloat16)
    att_f = attended.astype(jnp.float32)
    normed = (att_f * lax.rsqrt(lax.optimization_barrier(jnp.mean(att_f * att_f, axis=-1, keepdims=True)) + norm_eps) * norm_gain).astype(jnp.bfloat16)
    flat_routes = routes.reshape(-1)
    flat_gates = gate_probs.reshape(-1)
    bound_rows = WINDOW_TOKENS // MOE_DEV * CAP

    def expert_pass(accumulate, expert_id):
        hit_mask = flat_routes == expert_id
        picked_rows = jnp.nonzero(hit_mask, size=bound_rows, fill_value=0)[0].astype(jnp.int32)
        live_mask = jnp.arange(bound_rows, dtype=jnp.int32) < jnp.sum(hit_mask.astype(jnp.int32))
        token_ids = (picked_rows // TOPK).astype(jnp.int32)
        tokens_in = normed[token_ids]
        gate_h = jnp.dot(tokens_in, w_gate[expert_id], preferred_element_type=jnp.float32)
        up_h = jnp.dot(tokens_in, w_up[expert_id], preferred_element_type=jnp.float32)
        hidden = (jax.nn.silu(gate_h) * up_h).astype(jnp.bfloat16)
        produced = jnp.dot(hidden, w_down[expert_id], preferred_element_type=jnp.float32).astype(jnp.bfloat16)
        weight_col = jnp.where(live_mask, flat_gates[picked_rows], 0.0)
        accumulate = accumulate.at[token_ids].add(produced.astype(jnp.float32) * weight_col[:, None])
        return (accumulate, None)
    expert_mixture_sum, unused_out = lax.scan(expert_pass, jnp.zeros(att_f.shape, jnp.float32), jnp.arange(EXPERTS, dtype=jnp.int32))
    layer_out = (att_f + expert_mixture_sum).astype(jnp.bfloat16)
    return (attended, layer_out)
```

```python
import functools

import jax
import jax.numpy as jnp
from jax import lax
from jax.experimental import pallas as pl
from jax.experimental.pallas import tpu as pltpu
from jax.sharding import PartitionSpec as P

CG_STEPS = 4

exact_prec = lax.Precision.HIGHEST
norm_eps = 1e-06
BOTH = ("ctx", "head")


def grid_dims(count):
    bits = count.bit_length() - 1
    if 1 << bits != count:
        return (count, 1, 1)
    first = -(-bits // 3)
    second = -(-(bits - first) // 2)
    return (1 << first, 1 << second, 1 << (bits - first - second))


def shifted(place, dims, dim, by):
    coords = [place // (dims[1] * dims[2]), place // dims[2] % dims[1], place % dims[2]]
    coords[dim] = (coords[dim] + by) % dims[dim]
    return (coords[0] * dims[1] + coords[1]) * dims[2] + coords[2]


def phase_dims(dims):
    if dims[1] == dims[2]:
        return ((0, 2, 1), (0, 1, 2))
    return ((0, 2, 1), (0, 2, 1))


def hop(block, dims, n_head, phase, by):
    orders = phase_dims(dims)
    count = dims[0] * dims[1] * dims[2]
    pairs = []
    for place in range(count):
        for core in range(n_head):
            dest = shifted(place, dims, orders[core % 2][phase], by)
            pairs.append((place * n_head + core, dest * n_head + core))
    return lax.ppermute(block, BOTH, pairs)


def slot_sizes(dims):
    order = phase_dims(dims)[0]
    return tuple(dims[d] for d in order)


def spread(block, dims, n_head):
    s0, sa, sb = slot_sizes(dims)
    slots = {(0, 0, 0): block}
    for r0 in range(1, s0):
        slots[(r0, 0, 0)] = hop(block, dims, n_head, 0, r0)
    for r0 in range(s0):
        for ra in range(1, sa):
            slots[(r0, ra, 0)] = hop(slots[(r0, 0, 0)], dims, n_head, 1, ra)
        for rb in range(1, sb):
            slots[(r0, 0, rb)] = hop(slots[(r0, 0, 0)], dims, n_head, 2, rb)
    for r0 in range(s0):
        for ra in range(1, sa):
            for rb in range(1, sb):
                slots[(r0, ra, rb)] = hop(slots[(r0, ra, 0)], dims, n_head, 2, rb)
    return slots


def add_all(first, others, dtype):
    total = first.astype(jnp.float32)
    for other in others:
        total = total + other.astype(jnp.float32)
    return total.astype(dtype)


def collect(slots, dims, n_head):
    s0, sa, sb = slot_sizes(dims)
    lines = {}
    for r0 in range(s0):
        planes = {}
        for ra in list(range(1, sa)) + [0]:
            back = [hop(slots[(r0, ra, rb)], dims, n_head, 2, -rb) for rb in range(1, sb)]
            planes[ra] = add_all(slots[(r0, ra, 0)], back, jnp.bfloat16)
        back = [hop(planes[ra], dims, n_head, 1, -ra) for ra in range(1, sa)]
        lines[r0] = add_all(planes[0], back, jnp.bfloat16)
    return lines[0], [hop(lines[r0], dims, n_head, 0, -r0) for r0 in range(1, s0)]


def slot_source(key, dims):
    place = lax.axis_index("ctx")
    core = lax.axis_index("head") % 2
    orders = phase_dims(dims)
    sources = []
    for order in orders:
        coords = [place // (dims[1] * dims[2]), place // dims[2] % dims[1], place % dims[2]]
        for dim, by in zip(order, key, strict=True):
            coords[dim] = (coords[dim] - by) % dims[dim]
        sources.append((coords[0] * dims[1] + coords[1]) * dims[2] + coords[2])
    return jnp.where(core == 0, sources[0], sources[1]).astype(jnp.int32)


def expert_body(n_blocks, n_expert, cap, n_tiles, src_ref, slot_ref, gate_ref, *refs):
    blocks = refs[:n_blocks]
    gate_own, up_own, down_own, gate_oth, up_oth, down_oth = refs[n_blocks : n_blocks + 6]
    outs = refs[n_blocks + 6 : 2 * n_blocks + 6]
    picked, summed, scaled, select = refs[2 * n_blocks + 6 :]
    expert = pl.program_id(0)
    tile = pl.program_id(1)
    rows = n_blocks * cap
    tokens = blocks[0].shape[0]

    @pl.when((expert == 0) & (tile == 0))
    def _():
        for b in range(n_blocks):
            src = src_ref[b]
            for e in range(n_expert):
                wanted = slot_ref[src, pl.ds(e, 1), :]
                at = lax.broadcasted_iota(jnp.int32, (cap, tokens), 0)
                hit = (at == jnp.broadcast_to(wanted, (cap, tokens))).astype(jnp.float32)
                select[b, pl.ds(e * cap, cap), :] = hit.astype(jnp.bfloat16)
            got = jnp.dot(select[b], blocks[b][...], preferred_element_type=jnp.float32).astype(
                jnp.bfloat16
            )
            for e in range(n_expert):
                picked[e, pl.ds(b * cap, cap), :] = got[e * cap : (e + 1) * cap]

    def step(w_gate, w_up, w_down):
        tokens_in = picked[expert]
        gate_h = jnp.dot(tokens_in, w_gate[0], preferred_element_type=jnp.float32)
        up_h = jnp.dot(tokens_in, w_up[0], preferred_element_type=jnp.float32)
        hidden = (gate_h * (1.0 / (1.0 + jnp.exp(-gate_h))) * up_h).astype(jnp.bfloat16)
        part = jnp.dot(hidden, w_down[0], preferred_element_type=jnp.float32)

        @pl.when(tile == 0)
        def _():
            summed[...] = part

        @pl.when(tile > 0)
        def _():
            summed[...] += part

    @pl.when(expert < n_expert // 2)
    def _():
        step(gate_own, up_own, down_own)

    @pl.when(expert >= n_expert // 2)
    def _():
        step(gate_oth, up_oth, down_oth)

    @pl.when(tile == n_tiles - 1)
    def _():
        for b in range(n_blocks):
            src = src_ref[b]
            weight_row = gate_ref[src, pl.ds(expert, 1), :]
            hit = select[b, pl.ds(expert * cap, cap), :].astype(jnp.float32)
            weight = jnp.sum(hit * weight_row, axis=1, keepdims=True)
            scaled[b, pl.ds(expert * cap, cap), :] = (
                summed[pl.ds(b * cap, cap), :] * weight
            ).astype(jnp.bfloat16)

    @pl.when((tile == n_tiles - 1) & (expert == n_expert - 1))
    def _():
        for b in range(n_blocks):
            back = jnp.transpose(select[b].astype(jnp.float32)).astype(jnp.bfloat16)
            outs[b][...] = jnp.dot(back, scaled[b], preferred_element_type=jnp.float32).astype(
                jnp.bfloat16
            )


def run_experts(blocks, sources, slot_of, gate_of, own, other, cap):
    n_blocks = len(blocks)
    tokens, width = blocks[0].shape
    per_dev, _, hidden = own[0].shape
    n_expert = 2 * per_dev
    tile_f = 256 if hidden % 256 == 0 else hidden
    n_tiles = hidden // tile_f
    last = n_tiles - 1
    whole = lambda shape: pl.BlockSpec(
        shape, lambda e, f, s: (0,) * len(shape), pipeline_mode=pl.Buffered(1)
    )

    def own_at(e, f):
        here = e < per_dev
        return jnp.where(here, e, per_dev - 1), jnp.where(here, f, last)

    def other_at(e, f):
        here = e >= per_dev
        return jnp.where(here, e - per_dev, 0), jnp.where(here, f, 0)

    def in_spec(at):
        return pl.BlockSpec((1, width, tile_f), lambda e, f, s: (at(e, f)[0], 0, at(e, f)[1]))

    def out_spec(at):
        return pl.BlockSpec((1, tile_f, width), lambda e, f, s: (at(e, f)[0], at(e, f)[1], 0))

    rows = n_blocks * cap
    flops = 2 * n_expert * rows * width * hidden * 3
    moved = 2 * (2 * n_blocks * tokens * width + n_expert * 3 * width * hidden)
    return pl.pallas_call(
        functools.partial(expert_body, n_blocks, n_expert, cap, n_tiles),
        out_shape=[jax.ShapeDtypeStruct((tokens, width), jnp.bfloat16)] * n_blocks,
        grid_spec=pltpu.PrefetchScalarGridSpec(
            num_scalar_prefetch=1,
            grid=(n_expert, n_tiles),
            in_specs=[whole(slot_of.shape), whole(gate_of.shape)]
            + [whole((tokens, width))] * n_blocks
            + [in_spec(own_at), in_spec(own_at), out_spec(own_at)]
            + [in_spec(other_at), in_spec(other_at), out_spec(other_at)],
            out_specs=[whole((tokens, width))] * n_blocks,
            scratch_shapes=[
                pltpu.VMEM((n_expert, rows, width), jnp.bfloat16),
                pltpu.VMEM((rows, width), jnp.float32),
                pltpu.VMEM((n_blocks, n_expert * cap, width), jnp.bfloat16),
                pltpu.VMEM((n_blocks, n_expert * cap, tokens), jnp.bfloat16),
            ],
        ),
        compiler_params=pltpu.CompilerParams(
            dimension_semantics=("arbitrary", "arbitrary"), vmem_limit_bytes=60 * 1024 * 1024
        ),
        cost_estimate=pl.CostEstimate(
            flops=flops, bytes_accessed=moved, transcendentals=n_expert * rows * hidden
        ),
        name="experts",
    )(jnp.stack(sources), slot_of, gate_of, *blocks, *own, *other)


def unit_rows(vectors):
    floats = vectors.astype(jnp.float32)
    return floats * lax.rsqrt(jnp.sum(floats * floats, axis=-1, keepdims=True) + norm_eps)


def causal_weights(cumul_log):
    length = cumul_log.shape[1]
    lower_mask = jnp.arange(length)[:, None] >= jnp.arange(length)[None, :]
    gap_log = cumul_log[:, :, None] - cumul_log[:, None, :]
    return jnp.where(lower_mask[None], jnp.exp(jnp.where(lower_mask[None], gap_log, 0.0)), 0.0)


def apply_system(probe_vec, gram_prior, start_w, weights, key_f, ridge_diag):
    prior_part = start_w[:, :, None] * jnp.einsum(
        "hte,hde->htd", probe_vec, gram_prior, precision=exact_prec
    )
    scores = jnp.einsum("htd,hsd->hts", probe_vec, key_f, precision=exact_prec) * weights
    inner_part = jnp.einsum("hts,hsd->htd", scores, key_f, precision=exact_prec)
    return prior_part + inner_part + ridge_diag[:, None, :] * probe_vec


def conj_grad(rhs_vec, gram_prior, start_w, weights, key_f, ridge_diag):
    answer = jnp.zeros_like(rhs_vec)
    remain = rhs_vec
    direction = rhs_vec
    norm_now = jnp.sum(remain * remain, axis=-1)
    for step_id in range(CG_STEPS):
        applied = apply_system(direction, gram_prior, start_w, weights, key_f, ridge_diag)
        step_len = norm_now / jnp.sum(direction * applied, axis=-1)
        answer = answer + step_len[:, :, None] * direction
        remain = remain - step_len[:, :, None] * applied
        norm_next = jnp.sum(remain * remain, axis=-1)
        direction = remain + (norm_next / norm_now)[:, :, None] * direction
        norm_now = norm_next
    return answer


def flip_by(stack, place):
    count = stack.shape[0]
    bit = 1
    while bit < count:
        split = stack.reshape(count // (2 * bit), 2, bit, *stack.shape[1:])
        split = jnp.where((place & bit) != 0, split[:, ::-1], split)
        stack = split.reshape(stack.shape)
        bit *= 2
    return stack


def entering(tail_log, state, dims):
    heads, depth, width = state.shape
    plane = dims[1] * dims[2]
    n_ctx = dims[0] * plane
    place = lax.axis_index("ctx")
    mine = place % plane
    rows = heads * depth // plane
    pieces = state.reshape(plane, rows, width)
    tails = jnp.broadcast_to(tail_log[:, None], (heads, width))
    in_plane = lambda k: [
        (i, i // plane * plane + (i % plane ^ k)) for i in range(n_ctx)
    ]
    packed = []
    for k in range(plane):
        piece = lax.dynamic_index_in_dim(pieces, mine ^ k, 0, False)
        piece = jnp.concatenate([piece, tails], axis=0)
        packed.append(piece if k == 0 else lax.ppermute(piece, "ctx", in_plane(k)))
    got = jnp.stack([piece[:rows] for piece in packed])
    got_tails = jnp.stack([piece[rows:, 0] for piece in packed])
    ordered = flip_by(got_tails, mine)
    upto = jnp.cumsum(ordered, axis=0)
    at = jnp.arange(plane)
    upto_of = flip_by(upto, mine)
    before_of = flip_by(upto - ordered, mine)
    who = at ^ mine

    span = max(1, rows // depth)

    def per_row(by_head):
        first = mine * rows // depth
        part = lax.dynamic_slice_in_dim(by_head, first, span, axis=-1)
        part = jnp.broadcast_to(part[..., None], (*part.shape, rows // span))
        return part.reshape(*part.shape[:-2], rows)[..., None]

    total_tail = upto[-1]
    total = jnp.sum(per_row(jnp.exp(total_tail[None] - upto_of)) * got, axis=0)
    up = jnp.concatenate(
        [total, jnp.broadcast_to(total_tail[:, None], (heads, width))], axis=0
    )
    below = jnp.zeros_like(total)
    lost = jnp.zeros_like(total_tail)
    for r in range(1, dims[0]):
        pairs = [(i, i + r * plane) for i in range(n_ctx) if i + r * plane < n_ctx]
        came = lax.ppermute(up, "ctx", pairs)
        below = below + per_row(jnp.exp(lost)) * came[:rows]
        lost = lost + came[rows:, 0]
    result = []
    for k in range(plane):
        keep = (who < who[k])[:, None]
        gap = jnp.where(keep, before_of[k][None] - upto_of, 0.0)
        share = jnp.where(keep, jnp.exp(gap), 0.0)
        prior = per_row(jnp.exp(before_of[k])) * below + jnp.sum(per_row(share) * got, axis=0)
        result.append(prior if k == 0 else lax.ppermute(prior, "ctx", in_plane(k)))
    return flip_by(jnp.stack(result), mine).reshape(heads, depth, width)


def on_device(
    queries,
    key_vecs,
    values,
    log_decay,
    ridge_diag,
    residual,
    w_out,
    norm_gain,
    routes,
    gate_probs,
    w_gate,
    w_up,
    w_down,
):
    tok_dev, heads_dev, head_dim = queries.shape
    n_ctx = lax.axis_size("ctx")
    n_head = lax.axis_size("head")
    dims = grid_dims(n_ctx)
    core = lax.axis_index("head")
    swap = [(i, i ^ 1) for i in range(n_head)]

    tok_moe, top_count = routes.shape
    per_dev = w_gate.shape[0]
    expert_total = per_dev * n_ctx * n_head
    cap = 2 * tok_moe * top_count // expert_total
    own = (w_gate, w_up, w_down)
    other = tuple(lax.ppermute(w, "head", swap) for w in own)
    named = routes[:, :, None] == jnp.arange(expert_total, dtype=jnp.int32)[None, None, :]
    dense = jnp.sum(jnp.where(named, gate_probs[:, :, None], 0.0), axis=1)
    table = dense.T.reshape(n_ctx, n_head * per_dev, tok_moe)
    gate_of = lax.all_to_all(table, "ctx", split_axis=0, concat_axis=0, tiled=True)
    split = gate_of.reshape(n_ctx, n_head, per_dev, tok_moe)
    gate_of = jnp.where(core == 0, split, split[:, ::-1]).reshape(gate_of.shape)
    routed = (gate_of != 0.0).astype(jnp.bfloat16)
    earlier = (jnp.arange(tok_moe)[:, None] < jnp.arange(tok_moe)[None, :]).astype(jnp.bfloat16)
    before = jnp.einsum("set,tu->seu", routed, earlier, preferred_element_type=jnp.float32)
    slot_of = jnp.where(gate_of != 0.0, before.astype(jnp.int32), -1)

    query_unit = unit_rows(queries).transpose(1, 0, 2)
    key_narrow = lax.optimization_barrier(unit_rows(key_vecs).astype(jnp.bfloat16))
    key_f = key_narrow.astype(jnp.float32).transpose(1, 0, 2)
    value_f = values.astype(jnp.float32).transpose(1, 0, 2)
    cumul_log = jnp.cumsum(log_decay, axis=1)
    start_w = jnp.exp(cumul_log)
    end_w = jnp.exp(cumul_log[:, -1:] - cumul_log)[:, :, None]
    tail_log = cumul_log[:, -1]
    gram_loc = jnp.einsum("hsd,hse->hde", key_f * end_w, key_f, precision=exact_prec)
    value_loc = jnp.einsum("hse,hsd->hed", value_f * end_w, key_f, precision=exact_prec)
    gram_prior = entering(tail_log, gram_loc, dims)
    weights = causal_weights(cumul_log)
    value_prior = entering(tail_log, value_loc, dims)
    answer = conj_grad(query_unit, gram_prior, start_w, weights, key_f, ridge_diag)
    prior_part = start_w[:, :, None] * jnp.einsum(
        "htd,hed->hte", answer, value_prior, precision=exact_prec
    )
    scores = jnp.einsum("htd,hsd->hts", answer, key_f, precision=exact_prec) * weights
    mesa_out = prior_part + jnp.einsum("hts,hse->hte", scores, value_f, precision=exact_prec)
    mesa_rows = (
        mesa_out.astype(jnp.bfloat16).transpose(1, 0, 2).reshape(tok_dev, heads_dev * head_dim)
    )
    here = lax.dynamic_slice_in_dim(mesa_rows, core * tok_moe, tok_moe, 0)
    there = lax.dynamic_slice_in_dim(mesa_rows, (1 - core) * tok_moe, tok_moe, 0)
    sent = jnp.dot(there, w_out, preferred_element_type=jnp.float32).astype(jnp.bfloat16)
    came = lax.ppermute(sent, "head", swap)
    kept = jnp.dot(here, w_out, preferred_element_type=jnp.float32)
    attended = (residual.astype(jnp.float32) + kept + came.astype(jnp.float32)).astype(jnp.bfloat16)
    att_f = attended.astype(jnp.float32)
    normed = (
        att_f * lax.rsqrt(jnp.mean(att_f * att_f, axis=-1, keepdims=True) + norm_eps) * norm_gain
    ).astype(jnp.bfloat16)

    slots = spread(normed, dims, n_head)
    keys = list(slots)
    groups = [keys[: len(keys) // 2]]
    quarter = len(keys) // 4
    groups += [keys[len(keys) // 2 :][:quarter], keys[len(keys) // 2 :][quarter:]]
    limit = 8
    groups = [g[i : i + limit] for g in groups for i in range(0, len(g), limit)]
    produced = {}
    for group in groups:
        outs = run_experts(
            [slots[key] for key in group],
            [slot_source(key, dims) for key in group],
            slot_of,
            gate_of,
            own,
            other,
            cap,
        )
        produced.update(zip(group, outs, strict=True))
    first, rest = collect(produced, dims, n_head)
    layer_out = add_all(att_f + first.astype(jnp.float32), rest, jnp.bfloat16)
    return (attended, layer_out)


def solution(mesh):
    in_specs = (
        P("ctx", "head", None),
        P("ctx", "head", None),
        P("ctx", "head", None),
        P("head", "ctx"),
        P("head", None),
        P(("ctx", "head"), None),
        P("head", None),
        P(),
        P(("ctx", "head"), None),
        P(("ctx", "head"), None),
        P(("ctx", "head"), None, None),
        P(("ctx", "head"), None, None),
        P(("ctx", "head"), None, None),
    )
    out_specs = (P(("ctx", "head"), None), P(("ctx", "head"), None))
    return jax.shard_map(
        on_device, mesh=mesh, in_specs=in_specs, out_specs=out_specs, check_vma=False
    )
```

```python
import functools

import jax
import jax.numpy as jnp
from jax import lax
from jax.experimental import pallas as pl
from jax.experimental.pallas import tpu as pltpu
from jax.sharding import PartitionSpec as P

CG_STEPS = 4

exact_prec = lax.Precision.HIGHEST
norm_eps = 1e-06
BOTH = ("ctx", "head")


def grid_dims(count):
    bits = count.bit_length() - 1
    if 1 << bits != count:
        return (count, 1, 1)
    first = -(-bits // 3)
    second = -(-(bits - first) // 2)
    return (1 << first, 1 << second, 1 << (bits - first - second))


def shifted(place, dims, dim, by):
    coords = [place // (dims[1] * dims[2]), place // dims[2] % dims[1], place % dims[2]]
    coords[dim] = (coords[dim] + by) % dims[dim]
    return (coords[0] * dims[1] + coords[1]) * dims[2] + coords[2]


def phase_dims(dims):
    if dims[1] == dims[2]:
        return ((0, 2, 1), (0, 1, 2))
    return ((0, 2, 1), (0, 2, 1))


def hop(block, dims, n_head, phase, by):
    orders = phase_dims(dims)
    count = dims[0] * dims[1] * dims[2]
    pairs = []
    for place in range(count):
        for core in range(n_head):
            dest = shifted(place, dims, orders[core % 2][phase], by)
            pairs.append((place * n_head + core, dest * n_head + core))
    return lax.ppermute(block, BOTH, pairs)


def slot_sizes(dims):
    order = phase_dims(dims)[0]
    return tuple(dims[d] for d in order)


def spread(block, dims, n_head):
    s0, sa, sb = slot_sizes(dims)
    heads = [block]
    for r0 in visit(s0)[1:]:
        heads.append(hop(block, dims, n_head, 0, r0))
    groups = {}
    for r0, head in zip(visit(s0), heads, strict=True):
        line = [head]
        for ra in range(1, sa):
            line.append(hop(head, dims, n_head, 1, ra))
        group = [line]
        for rb in range(1, sb):
            group.append([hop(one, dims, n_head, 2, rb) for one in line])
        groups[r0] = group
    return groups


def visit(size):
    return sorted(range(size), key=lambda r: (min(r, size - r), r))


def add_all(first, others, dtype):
    total = first.astype(jnp.float32)
    for other in others:
        total = total + other.astype(jnp.float32)
    return total.astype(dtype)


def collect(outs, r0, dims, n_head):
    _, sa, sb = slot_sizes(dims)
    rows = outs[0].shape[0] // sa
    came = []
    for rb in range(1, sb):
        came.append(hop(outs[rb], dims, n_head, 2, -rb))
    part = lambda array, ra: array[ra * rows : (ra + 1) * rows]
    line = []
    for ra in range(1, sa):
        total = add_all(part(outs[0], ra), [part(c, ra) for c in came], jnp.bfloat16)
        line.append(hop(total, dims, n_head, 1, -ra))
    total = add_all(part(outs[0], 0), [part(c, 0) for c in came] + line, jnp.bfloat16)
    if r0 == 0:
        return total
    return hop(total, dims, n_head, 0, -r0)


def slot_source(key, dims):
    place = lax.axis_index("ctx")
    core = lax.axis_index("head") % 2
    orders = phase_dims(dims)
    sources = []
    for order in orders:
        coords = [place // (dims[1] * dims[2]), place // dims[2] % dims[1], place % dims[2]]
        for dim, by in zip(order, key, strict=True):
            coords[dim] = (coords[dim] - by) % dims[dim]
        sources.append((coords[0] * dims[1] + coords[1]) * dims[2] + coords[2])
    return jnp.where(core == 0, sources[0], sources[1]).astype(jnp.int32)


def expert_body(n_a, n_b, n_expert, cap, n_tiles, src_ref, slot_ref, gate_ref, *refs):
    n_blocks = n_a * n_b
    blocks = refs[:n_blocks]
    gate_own, up_own, down_own, gate_oth, up_oth, down_oth = refs[n_blocks : n_blocks + 6]
    outs = refs[n_blocks + 6 : n_blocks + 6 + n_b]
    picked, hidden_of, scaled, select = refs[n_blocks + 6 + n_b :]
    expert = pl.program_id(0)
    tile = pl.program_id(1)
    tokens = blocks[0].shape[0]

    @pl.when((expert == 0) & (tile == 0))
    def _():
        for b in range(n_blocks):
            src = src_ref[b]
            for e in range(n_expert):
                wanted = slot_ref[src, pl.ds(e, 1), :]
                at = lax.broadcasted_iota(jnp.int32, (cap, tokens), 0)
                hit = (at == jnp.broadcast_to(wanted, (cap, tokens))).astype(jnp.float32)
                select[b, pl.ds(e * cap, cap), :] = hit.astype(jnp.bfloat16)
            got = jnp.dot(select[b], blocks[b][...], preferred_element_type=jnp.float32).astype(
                jnp.bfloat16
            )
            for e in range(n_expert):
                picked[e, pl.ds(b * cap, cap), :] = got[e * cap : (e + 1) * cap]

    def step(w_gate, w_up):
        tokens_in = picked[expert]
        gate_h = jnp.dot(tokens_in, w_gate[0], preferred_element_type=jnp.float32)
        up_h = jnp.dot(tokens_in, w_up[0], preferred_element_type=jnp.float32)
        hidden = gate_h * (1.0 / (1.0 + jnp.exp(-gate_h))) * up_h
        hidden_of[tile] = hidden.astype(jnp.bfloat16)

    def finish(w_down):
        hidden = jnp.concatenate([hidden_of[i] for i in range(n_tiles)], axis=1)
        result = jnp.dot(hidden, w_down[0], preferred_element_type=jnp.float32)
        for b in range(n_blocks):
            src = src_ref[b]
            weight_row = gate_ref[src, pl.ds(expert, 1), :]
            hit = select[b, pl.ds(expert * cap, cap), :].astype(jnp.float32)
            weight = jnp.sum(hit * weight_row, axis=1, keepdims=True)
            scaled[b, pl.ds(expert * cap, cap), :] = (
                result[b * cap : (b + 1) * cap] * weight
            ).astype(jnp.bfloat16)

    @pl.when(expert < n_expert // 2)
    def _():
        step(gate_own, up_own)

        @pl.when(tile == n_tiles - 1)
        def _():
            finish(down_own)

    @pl.when(expert >= n_expert // 2)
    def _():
        step(gate_oth, up_oth)

        @pl.when(tile == n_tiles - 1)
        def _():
            finish(down_oth)

    @pl.when((tile == n_tiles - 1) & (expert == n_expert - 1))
    def _():
        for b in range(n_blocks):
            back = jnp.transpose(select[b].astype(jnp.float32)).astype(jnp.bfloat16)
            outs[b // n_a][pl.ds(b % n_a * tokens, tokens), :] = jnp.dot(
                back, scaled[b], preferred_element_type=jnp.float32
            ).astype(jnp.bfloat16)


def run_experts(group, sources, slot_of, gate_of, own, other, cap):
    n_b, n_a = len(group), len(group[0])
    blocks = [block for line in group for block in line]
    n_blocks = len(blocks)
    tokens, width = blocks[0].shape
    per_dev, _, hidden = own[0].shape
    n_expert = 2 * per_dev
    tile_f = 256 if hidden % 256 == 0 else hidden
    n_tiles = hidden // tile_f
    last = n_tiles - 1
    whole = lambda shape: pl.BlockSpec(
        shape, lambda e, f, s: (0,) * len(shape), pipeline_mode=pl.Buffered(1)
    )

    def own_at(e, f):
        here = e < per_dev
        return jnp.where(here, e, per_dev - 1), jnp.where(here, f, last)

    def other_at(e, f):
        here = e >= per_dev
        return jnp.where(here, e - per_dev, 0), jnp.where(here, f, 0)

    def in_spec(at):
        return pl.BlockSpec((1, width, tile_f), lambda e, f, s: (at(e, f)[0], 0, at(e, f)[1]))

    def out_spec(at):
        return pl.BlockSpec((1, hidden, width), lambda e, f, s: (at(e, f)[0], 0, 0))

    rows = n_blocks * cap
    flops = 2 * n_expert * rows * width * hidden * 3
    moved = 2 * (2 * n_blocks * tokens * width + n_expert * 3 * width * hidden)
    return pl.pallas_call(
        functools.partial(expert_body, n_a, n_b, n_expert, cap, n_tiles),
        out_shape=[jax.ShapeDtypeStruct((n_a * tokens, width), jnp.bfloat16)] * n_b,
        grid_spec=pltpu.PrefetchScalarGridSpec(
            num_scalar_prefetch=1,
            grid=(n_expert, n_tiles),
            in_specs=[whole(slot_of.shape), whole(gate_of.shape)]
            + [whole((tokens, width))] * n_blocks
            + [in_spec(own_at), in_spec(own_at), out_spec(own_at)]
            + [in_spec(other_at), in_spec(other_at), out_spec(other_at)],
            out_specs=[whole((n_a * tokens, width))] * n_b,
            scratch_shapes=[
                pltpu.VMEM((n_expert, rows, width), jnp.bfloat16),
                pltpu.VMEM((n_tiles, rows, tile_f), jnp.bfloat16),
                pltpu.VMEM((n_blocks, n_expert * cap, width), jnp.bfloat16),
                pltpu.VMEM((n_blocks, n_expert * cap, tokens), jnp.bfloat16),
            ],
        ),
        compiler_params=pltpu.CompilerParams(
            dimension_semantics=("arbitrary", "arbitrary"), vmem_limit_bytes=60 * 1024 * 1024
        ),
        cost_estimate=pl.CostEstimate(
            flops=flops, bytes_accessed=moved, transcendentals=n_expert * rows * hidden
        ),
    )(sources, slot_of, gate_of, *blocks, *own, *other)


def unit_rows(vectors):
    floats = vectors.astype(jnp.float32)
    return floats * lax.rsqrt(jnp.sum(floats * floats, axis=-1, keepdims=True) + norm_eps)


def causal_weights(cumul_log):
    length = cumul_log.shape[1]
    lower_mask = jnp.arange(length)[:, None] >= jnp.arange(length)[None, :]
    gap_log = cumul_log[:, :, None] - cumul_log[:, None, :]
    return jnp.where(lower_mask[None], jnp.exp(jnp.where(lower_mask[None], gap_log, 0.0)), 0.0)


def apply_system(probe_vec, gram_prior, start_w, weights, key_f, ridge_diag):
    prior_part = start_w[:, :, None] * jnp.einsum(
        "hte,hde->htd", probe_vec, gram_prior, precision=exact_prec
    )
    scores = jnp.einsum("htd,hsd->hts", probe_vec, key_f, precision=exact_prec) * weights
    inner_part = jnp.einsum("hts,hsd->htd", scores, key_f, precision=exact_prec)
    return prior_part + inner_part + ridge_diag[:, None, :] * probe_vec


def conj_grad(rhs_vec, gram_prior, start_w, weights, key_f, ridge_diag):
    answer = jnp.zeros_like(rhs_vec)
    remain = rhs_vec
    direction = rhs_vec
    norm_now = jnp.sum(remain * remain, axis=-1)
    for _ in range(CG_STEPS):
        applied = apply_system(direction, gram_prior, start_w, weights, key_f, ridge_diag)
        step_len = norm_now / jnp.sum(direction * applied, axis=-1)
        answer = answer + step_len[:, :, None] * direction
        remain = remain - step_len[:, :, None] * applied
        norm_next = jnp.sum(remain * remain, axis=-1)
        direction = remain + (norm_next / norm_now)[:, :, None] * direction
        norm_now = norm_next
    return answer


def flip_by(stack, place):
    count = stack.shape[0]
    bit = 1
    while bit < count:
        split = stack.reshape(count // (2 * bit), 2, bit, *stack.shape[1:])
        split = jnp.where((place & bit) != 0, split[:, ::-1], split)
        stack = split.reshape(stack.shape)
        bit *= 2
    return stack


def split_three(exact):
    terms = []
    for _ in range(3):
        term = lax.reduce_precision(exact, 8, 7)
        terms.append(term.astype(jnp.bfloat16))
        exact = exact - term
    return terms


def entering(tail_log, state, dims, link, aside):
    heads, depth, width = state.shape
    plane = dims[1] * dims[2]
    n_ctx = dims[0] * plane
    place = lax.axis_index("ctx")
    mine = place % plane
    rows = heads * depth // plane
    pieces = state.reshape(plane, rows, width).astype(link)

    def with_tail(piece, tail):
        terms = jnp.stack(split_three(tail), axis=1)
        terms = jnp.pad(terms, ((0, 0), (0, width - 3))).astype(link)
        return jnp.concatenate([piece, terms], axis=0)

    def without_tail(packed):
        packed = packed.astype(jnp.float32)
        return packed[:rows], jnp.sum(packed[rows:, :3], axis=1)

    in_plane = lambda k: [
        (i, i // plane * plane + (i % plane ^ k)) for i in range(n_ctx)
    ]
    got, got_tails = [], []
    for k in range(plane):
        packed = with_tail(lax.dynamic_index_in_dim(pieces, mine ^ k, 0, False), tail_log)
        if k:
            packed = lax.ppermute(packed, "ctx", in_plane(k))
        piece, tail = without_tail(packed)
        got.append(piece)
        got_tails.append(tail)
    got = jnp.stack(got)
    ordered = flip_by(jnp.stack(got_tails), mine)
    upto = jnp.cumsum(ordered, axis=0)
    upto_of = flip_by(upto, mine)
    before_of = flip_by(upto - ordered, mine)
    who = jnp.arange(plane) ^ mine
    span = max(1, rows // depth)

    def per_row(by_head):
        first = mine * rows // depth
        part = lax.dynamic_slice_in_dim(by_head, first, span, axis=-1)
        part = jnp.broadcast_to(part[..., None], (*part.shape, rows // span))
        return part.reshape(*part.shape[:-2], rows, 1)

    total_tail = upto[-1]
    total = jnp.sum(per_row(jnp.exp(total_tail[None] - upto_of)) * got, axis=0)
    up = with_tail(total.astype(link), total_tail)
    up, aside = lax.optimization_barrier((up, aside))
    below = jnp.zeros_like(total)
    lost = jnp.zeros_like(total_tail)
    for r in range(1, dims[0]):
        pairs = [(i, i + r * plane) for i in range(n_ctx) if i + r * plane < n_ctx]
        came = lax.ppermute(up, "ctx", pairs)
        piece, tail = without_tail(came)
        below = below + per_row(jnp.exp(lost)) * piece
        lost = lost + tail
    result = []
    for k in range(plane):
        keep = (who < who[k])[:, None]
        gap = jnp.where(keep, before_of[k][None] - upto_of, 0.0)
        share = jnp.where(keep, jnp.exp(gap), 0.0)
        prior = per_row(jnp.exp(before_of[k])) * below + jnp.sum(per_row(share) * got, axis=0)
        prior = prior.astype(link)
        if k:
            prior = lax.ppermute(prior, "ctx", in_plane(k))
        result.append(prior)
    result = flip_by(jnp.stack(result), mine)
    return result.reshape(heads, depth, width).astype(jnp.float32), aside


def on_device(
    queries,
    key_vecs,
    values,
    log_decay,
    ridge_diag,
    residual,
    w_out,
    norm_gain,
    routes,
    gate_probs,
    w_gate,
    w_up,
    w_down,
):
    tok_dev, heads_dev, head_dim = queries.shape
    n_ctx = lax.axis_size("ctx")
    n_head = lax.axis_size("head")
    dims = grid_dims(n_ctx)
    core = lax.axis_index("head")
    swap = [(i, i ^ 1) for i in range(n_head)]

    tok_moe, top_count = routes.shape
    per_dev = w_gate.shape[0]
    expert_total = per_dev * n_ctx * n_head
    cap = 2 * tok_moe * top_count // expert_total
    own = (w_gate, w_up, w_down)
    other = tuple(lax.ppermute(w, "head", swap) for w in own)
    named = routes[:, :, None] == jnp.arange(expert_total, dtype=jnp.int32)[None, None, :]
    dense = jnp.sum(jnp.where(named, gate_probs[:, :, None], 0.0), axis=1)
    table = dense.T.reshape(n_ctx, n_head * per_dev, tok_moe)
    query_unit = unit_rows(queries).transpose(1, 0, 2)
    key_narrow = lax.optimization_barrier(unit_rows(key_vecs).astype(jnp.bfloat16))
    key_f = key_narrow.astype(jnp.float32).transpose(1, 0, 2)
    value_f = values.astype(jnp.float32).transpose(1, 0, 2)
    cumul_log = jnp.cumsum(log_decay, axis=1)
    start_w = jnp.exp(cumul_log)
    end_w = jnp.exp(cumul_log[:, -1:] - cumul_log)[:, :, None]
    tail_log = cumul_log[:, -1]
    gram_loc = jnp.einsum("hsd,hse->hde", key_f * end_w, key_f, precision=exact_prec)
    value_loc = jnp.einsum("hse,hsd->hed", value_f * end_w, key_f, precision=exact_prec)
    weights = causal_weights(cumul_log)
    gram_prior, table = entering(tail_log, gram_loc, dims, jnp.float32, table)
    value_prior, _ = entering(tail_log, value_loc, dims, jnp.bfloat16, ())
    gate_of = lax.all_to_all(table, "ctx", split_axis=0, concat_axis=0, tiled=True)
    split = gate_of.reshape(n_ctx, n_head, per_dev, tok_moe)
    gate_of = jnp.where(core == 0, split, split[:, ::-1]).reshape(gate_of.shape)
    routed = (gate_of != 0.0).astype(jnp.bfloat16)
    earlier = (jnp.arange(tok_moe)[:, None] < jnp.arange(tok_moe)[None, :]).astype(jnp.bfloat16)
    before = jnp.einsum("set,tu->seu", routed, earlier, preferred_element_type=jnp.float32)
    slot_of = jnp.where(gate_of != 0.0, before.astype(jnp.int32), -1)

    gram_prior, gate_of = lax.optimization_barrier((gram_prior, gate_of))
    answer = conj_grad(query_unit, gram_prior, start_w, weights, key_f, ridge_diag)
    prior_part = start_w[:, :, None] * jnp.einsum(
        "htd,hed->hte", answer, value_prior, precision=exact_prec
    )
    scores = jnp.einsum("htd,hsd->hts", answer, key_f, precision=exact_prec) * weights
    mesa_out = prior_part + jnp.einsum("hts,hse->hte", scores, value_f, precision=exact_prec)
    mesa_rows = (
        mesa_out.astype(jnp.bfloat16).transpose(1, 0, 2).reshape(tok_dev, heads_dev * head_dim)
    )
    here = lax.dynamic_slice_in_dim(mesa_rows, core * tok_moe, tok_moe, 0)
    there = lax.dynamic_slice_in_dim(mesa_rows, (1 - core) * tok_moe, tok_moe, 0)
    sent = jnp.dot(there, w_out, preferred_element_type=jnp.float32).astype(jnp.bfloat16)
    came = lax.ppermute(sent, "head", swap)
    kept = jnp.dot(here, w_out, preferred_element_type=jnp.float32)
    attended = (residual.astype(jnp.float32) + kept + came.astype(jnp.float32)).astype(jnp.bfloat16)
    att_f = attended.astype(jnp.float32)
    normed = (
        att_f * lax.rsqrt(jnp.mean(att_f * att_f, axis=-1, keepdims=True) + norm_eps) * norm_gain
    ).astype(jnp.bfloat16)

    groups = spread(normed, dims, n_head)
    back = []
    for r0, group in groups.items():
        sources = [
            slot_source((r0, ra, rb), dims) for rb in range(len(group)) for ra in range(len(group[0]))
        ]
        sources = lax.optimization_barrier(jnp.stack(sources))
        outs = run_experts(group, sources, slot_of, gate_of, own, other, cap)
        back.append(collect(outs, r0, dims, n_head))
    layer_out = add_all(att_f, back, jnp.bfloat16)
    return (attended, layer_out)


def solution(mesh):
    in_specs = (
        P("ctx", "head", None),
        P("ctx", "head", None),
        P("ctx", "head", None),
        P("head", "ctx"),
        P("head", None),
        P(("ctx", "head"), None),
        P("head", None),
        P(),
        P(("ctx", "head"), None),
        P(("ctx", "head"), None),
        P(("ctx", "head"), None, None),
        P(("ctx", "head"), None, None),
        P(("ctx", "head"), None, None),
    )
    out_specs = (P(("ctx", "head"), None), P(("ctx", "head"), None))

    return jax.shard_map(
        on_device, mesh=mesh, in_specs=in_specs, out_specs=out_specs, check_vma=False
    )
```

```python
import functools

import jax
import jax.numpy as jnp
from jax import lax
from jax.experimental import pallas as pl
from jax.experimental.pallas import tpu as pltpu
from jax.sharding import PartitionSpec as P

CG_STEPS = 4

norm_eps = 1e-06
BOTH = ("ctx", "head")


def grid_dims(count):
    bits = count.bit_length() - 1
    if 1 << bits != count:
        return (count, 1, 1)
    first = -(-bits // 3)
    second = -(-(bits - first) // 2)
    return (1 << first, 1 << second, 1 << (bits - first - second))


def shifted(place, dims, dim, by):
    coords = [place // (dims[1] * dims[2]), place // dims[2] % dims[1], place % dims[2]]
    coords[dim] = (coords[dim] + by) % dims[dim]
    return (coords[0] * dims[1] + coords[1]) * dims[2] + coords[2]


def phase_dims(dims):
    if dims[1] == dims[2]:
        return ((0, 2, 1), (0, 1, 2))
    return ((0, 2, 1), (0, 2, 1))


def hop(block, dims, n_head, phase, by):
    orders = phase_dims(dims)
    count = dims[0] * dims[1] * dims[2]
    pairs = []
    for place in range(count):
        for core in range(n_head):
            dest = shifted(place, dims, orders[core % 2][phase], by)
            pairs.append((place * n_head + core, dest * n_head + core))
    return lax.ppermute(block, BOTH, pairs)


def slot_sizes(dims):
    order = phase_dims(dims)[0]
    return tuple(dims[d] for d in order)


def spread(block, dims, n_head):
    s0, sa, sb = slot_sizes(dims)
    heads = [block]
    for r0 in visit(s0)[1:]:
        heads.append(hop(block, dims, n_head, 0, r0))
    groups = {}
    for r0, head in zip(visit(s0), heads, strict=True):
        line = [head]
        for ra in range(1, sa):
            line.append(hop(head, dims, n_head, 1, ra))
        group = [line]
        for rb in range(1, sb):
            group.append([hop(one, dims, n_head, 2, rb) for one in line])
        groups[r0] = group
    return groups


def visit(size):
    return sorted(range(size), key=lambda r: (min(r, size - r), r))


def call_order(size):
    return visit(size)[1:] + [0]


def add_all(first, others, dtype):
    total = first.astype(jnp.float32)
    for other in others:
        total = total + other.astype(jnp.float32)
    return total.astype(dtype)


def collect(outs, r0, dims, n_head):
    _, sa, sb = slot_sizes(dims)
    rows = outs[0].shape[0] // sa
    came = []
    for rb in range(1, sb):
        came.append(hop(outs[rb], dims, n_head, 2, -rb))
    part = lambda array, ra: array[ra * rows : (ra + 1) * rows]
    line = []
    for ra in range(1, sa):
        total = add_all(part(outs[0], ra), [part(c, ra) for c in came], jnp.bfloat16)
        line.append(hop(total, dims, n_head, 1, -ra))
    total = add_all(part(outs[0], 0), [part(c, 0) for c in came] + line, jnp.bfloat16)
    if r0 == 0:
        return total
    return hop(total, dims, n_head, 0, -r0)


def slot_source(key, dims):
    place = lax.axis_index("ctx")
    core = lax.axis_index("head") % 2
    orders = phase_dims(dims)
    sources = []
    for order in orders:
        coords = [place // (dims[1] * dims[2]), place // dims[2] % dims[1], place % dims[2]]
        for dim, by in zip(order, key, strict=True):
            coords[dim] = (coords[dim] - by) % dims[dim]
        sources.append((coords[0] * dims[1] + coords[1]) * dims[2] + coords[2])
    return jnp.where(core == 0, sources[0], sources[1]).astype(jnp.int32)


def expert_body(n_a, n_b, n_expert, cap, parts, src_ref, slot_ref, gate_ref, *refs):
    n_blocks = n_a * n_b
    blocks = refs[:n_blocks]
    weights = refs[n_blocks : n_blocks + 6]
    outs = refs[n_blocks + 6 : n_blocks + 6 + n_b]
    x_buf, *w_bufs, picked, scaled, select, x_sem, w_sem = refs[n_blocks + 6 + n_b :]
    tokens = blocks[0].shape[0]
    per_dev = n_expert // 2

    x_copies = [
        pltpu.make_async_copy(block, x_buf.at[b], x_sem.at[b]) for b, block in enumerate(blocks)
    ]
    w_copies = {}
    for e in range(n_expert):
        side, place = divmod(e, per_dev)
        for kind in range(3):
            source = weights[3 * side + kind]
            size = source.shape[1] // parts
            w_copies[e, kind] = [
                pltpu.make_async_copy(
                    source.at[place, pl.ds(i * size, size)],
                    w_bufs[kind].at[e, pl.ds(i * size, size)],
                    w_sem.at[3 * e + kind, i],
                )
                for i in range(parts)
            ]
    for copy in x_copies:
        copy.start()
    for group in w_copies.values():
        for copy in group:
            copy.start()

    def ready(e, kind):
        for copy in w_copies[e, kind]:
            copy.wait()
        return w_bufs[kind][e]

    for b in range(n_blocks):
        src = src_ref[b]
        for e in range(n_expert):
            wanted = slot_ref[src, e : e + 1, :]
            at = lax.broadcasted_iota(jnp.int32, (cap, tokens), 0)
            hit = (at == jnp.broadcast_to(wanted, (cap, tokens))).astype(jnp.float32)
            select[b, e * cap : (e + 1) * cap, :] = hit.astype(jnp.bfloat16)
        x_copies[b].wait()
        got = jnp.dot(select[b], x_buf[b], preferred_element_type=jnp.float32)
        got = got.astype(jnp.bfloat16)
        for e in range(n_expert):
            picked[e, b * cap : (b + 1) * cap, :] = got[e * cap : (e + 1) * cap]

    for e in range(n_expert):
        tokens_in = picked[e]
        gate_h = jnp.dot(tokens_in, ready(e, 0), preferred_element_type=jnp.float32)
        up_h = jnp.dot(tokens_in, ready(e, 1), preferred_element_type=jnp.float32)
        hidden = (gate_h * (1.0 / (1.0 + jnp.exp(-gate_h))) * up_h).astype(jnp.bfloat16)
        result = jnp.dot(hidden, ready(e, 2), preferred_element_type=jnp.float32)
        for b in range(n_blocks):
            weight_row = gate_ref[src_ref[b], e : e + 1, :]
            hit = select[b, e * cap : (e + 1) * cap, :].astype(jnp.float32)
            weight = jnp.sum(hit * weight_row, axis=1, keepdims=True)
            part = result[b * cap : (b + 1) * cap] * weight
            scaled[b, e * cap : (e + 1) * cap, :] = part.astype(jnp.bfloat16)

    for b in range(n_blocks):
        back = jnp.transpose(select[b].astype(jnp.float32)).astype(jnp.bfloat16)
        total = jnp.dot(back, scaled[b], preferred_element_type=jnp.float32)
        first = b % n_a * tokens
        outs[b // n_a][first : first + tokens, :] = total.astype(jnp.bfloat16)


def run_experts(group, sources, slot_of, gate_of, own, other, cap):
    n_b, n_a = len(group), len(group[0])
    blocks = [block for line in group for block in line]
    n_blocks = len(blocks)
    tokens, width = blocks[0].shape
    per_dev, _, hidden = own[0].shape
    n_expert = 2 * per_dev
    parts = 2
    whole = lambda shape: pl.BlockSpec(shape, lambda i, s: (0,) * len(shape))
    apart = pl.BlockSpec(memory_space=pl.ANY)
    rows = n_blocks * cap
    flops = 2 * n_expert * rows * width * hidden * 3
    moved = 2 * (2 * n_blocks * tokens * width + n_expert * 3 * width * hidden)
    return pl.pallas_call(
        functools.partial(expert_body, n_a, n_b, n_expert, cap, parts),
        out_shape=[jax.ShapeDtypeStruct((n_a * tokens, width), jnp.bfloat16)] * n_b,
        grid_spec=pltpu.PrefetchScalarGridSpec(
            num_scalar_prefetch=1,
            grid=(1,),
            in_specs=[whole(slot_of.shape), whole(gate_of.shape)] + [apart] * (n_blocks + 6),
            out_specs=[whole((n_a * tokens, width))] * n_b,
            scratch_shapes=[
                pltpu.VMEM((n_blocks, tokens, width), jnp.bfloat16),
                pltpu.VMEM((n_expert, width, hidden), jnp.bfloat16),
                pltpu.VMEM((n_expert, width, hidden), jnp.bfloat16),
                pltpu.VMEM((n_expert, hidden, width), jnp.bfloat16),
                pltpu.VMEM((n_expert, rows, width), jnp.bfloat16),
                pltpu.VMEM((n_blocks, n_expert * cap, width), jnp.bfloat16),
                pltpu.VMEM((n_blocks, n_expert * cap, tokens), jnp.bfloat16),
                pltpu.SemaphoreType.DMA((n_blocks,)),
                pltpu.SemaphoreType.DMA((3 * n_expert, parts)),
            ],
        ),
        compiler_params=pltpu.CompilerParams(vmem_limit_bytes=60 * 1024 * 1024),
        cost_estimate=pl.CostEstimate(
            flops=flops, bytes_accessed=moved, transcendentals=n_expert * rows * hidden
        ),
    )(sources, slot_of, gate_of, *blocks, *own, *other)


def two_terms(exact):
    high = exact.astype(jnp.bfloat16)
    return high, (exact - high.astype(jnp.float32)).astype(jnp.bfloat16)


def mm(lhs, rhs, at_lhs, at_rhs):
    return lax.dot_general(
        lhs, rhs, (((at_lhs,), (at_rhs,)), ((), ())), preferred_element_type=jnp.float32
    )


def mm_split(exact, narrow, at_lhs, at_rhs):
    high, low = two_terms(exact)
    return mm(high, narrow, at_lhs, at_rhs) + mm(low, narrow, at_lhs, at_rhs)


def unit_rows(vectors):
    floats = vectors.astype(jnp.float32)
    return floats * lax.rsqrt(jnp.sum(floats * floats, axis=-1, keepdims=True) + norm_eps)


def down_rows(row, lanes):
    return jnp.transpose(jnp.broadcast_to(row, (lanes, row.shape[1])))


def prep_body(rows, key_ref, value_ref, cumul_ref, unit_ref, gram_ref, held_ref):
    heads, length, depth = key_ref.shape
    last = cumul_ref[:, length - 1 : length]
    chunk = min(rows, depth)
    for h in range(heads):
        unit = unit_rows(key_ref[h]).astype(jnp.bfloat16)
        unit_ref[h] = unit
        left = last[h : h + 1] - cumul_ref[h : h + 1, :]
        faded = unit.astype(jnp.float32) * jnp.exp(down_rows(left, depth))
        high, low = two_terms(faded)
        gram = mm(high, unit, 0, 0) + mm(low, unit, 0, 0)
        held = mm(value_ref[h], high, 0, 0) + mm(value_ref[h], low, 0, 0)
        for start in range(0, depth, chunk):
            piece, at = divmod(h * depth + start, rows)
            gram_ref[piece, at : at + chunk, :] = gram[start : start + chunk]
            held_ref[piece, at : at + chunk, :] = held[start : start + chunk].astype(held_ref.dtype)
    tails = jnp.broadcast_to(last, (heads, depth))
    for piece in range(gram_ref.shape[0]):
        gram_ref[piece, rows : rows + heads, :] = tails


def prep(keys, values, cumul_log, plane):
    heads, length, depth = keys.shape
    rows = heads * depth // plane
    return pl.pallas_call(
        functools.partial(prep_body, rows),
        out_shape=[
            jax.ShapeDtypeStruct(keys.shape, jnp.bfloat16),
            jax.ShapeDtypeStruct((plane, rows + heads, depth), jnp.float32),
            jax.ShapeDtypeStruct((plane, rows, depth), jnp.bfloat16),
        ],
        cost_estimate=pl.CostEstimate(
            flops=8 * heads * length * depth * depth,
            bytes_accessed=8 * heads * length * depth,
            transcendentals=heads * length * depth,
        ),
        name="prep",
    )(keys, values, cumul_log)


def plane_sums(tails, mine):
    count = len(tails)
    upto, before = [], []
    for k in range(count):
        total = jnp.zeros_like(tails[0])
        for j in range(count):
            total = total + jnp.where((mine ^ j) < (mine ^ k), tails[j], 0.0)
        before.append(total)
        upto.append(total + tails[k])
    return upto, before, functools.reduce(lambda x, y: x + y, tails)


def by_row(factors, table_ref, mine, rows, depth):
    table_ref[...] = factors
    span = max(1, rows // depth)
    first = mine * rows // depth
    return [table_ref[pl.ds(first + i, 1), :] for i in range(span)]


def weighted(factors, piece_ref, rows):
    step = rows // len(factors)
    return [
        f * piece_ref[i * step : (i + 1) * step, :].astype(jnp.float32)
        for i, f in enumerate(factors)
    ]


def mid_body(count, rows, tailed, mine_ref, *refs):
    pieces, tail_refs, up_ref, table_ref = refs[:count], refs[count : -2], refs[-2], refs[-1]
    heads, depth = table_ref.shape
    mine = mine_ref[0]
    tails = [t[...] for t in tail_refs]
    upto, _, every = plane_sums(tails, mine)
    total = None
    for k in range(count):
        factors = by_row(jnp.exp(every - upto[k]), table_ref, mine, rows, depth)
        term = weighted(factors, pieces[k], rows)
        total = term if total is None else [x + y for x, y in zip(total, term, strict=True)]
    step = rows // len(total)
    for i, part in enumerate(total):
        up_ref[i * step : (i + 1) * step, :] = part.astype(up_ref.dtype)
    if tailed:
        up_ref[rows : rows + heads, :] = every


def post_body(count, shifts, rows, mine_ref, *refs):
    pieces, tail_refs = refs[:count], refs[count : 2 * count]
    came = refs[2 * count : 2 * count + shifts]
    came_tails = refs[2 * count + shifts : 2 * count + 2 * shifts]
    outs, table_ref = refs[2 * count + 2 * shifts : -1], refs[-1]
    heads, depth = table_ref.shape
    mine = mine_ref[0]
    upto, before, _ = plane_sums([t[...] for t in tail_refs], mine)
    lost = jnp.zeros((heads, depth), jnp.float32)
    below = None
    for r in range(shifts):
        factors = by_row(jnp.exp(lost), table_ref, mine, rows, depth)
        term = weighted(factors, came[r], rows)
        below = term if below is None else [x + y for x, y in zip(below, term, strict=True)]
        lost = lost + came_tails[r][...]
    for k in range(count):
        factors = by_row(jnp.exp(before[k]), table_ref, mine, rows, depth)
        if below is None:
            total = [jnp.zeros((rows // len(factors), depth), jnp.float32)] * len(factors)
        else:
            total = [f * part for f, part in zip(factors, below, strict=True)]
        for j in range(count):
            if j == k:
                continue
            earlier = (mine ^ j) < (mine ^ k)
            share = jnp.where(earlier, jnp.exp(jnp.where(earlier, before[k] - upto[j], 0.0)), 0.0)
            factors = by_row(share, table_ref, mine, rows, depth)
            term = weighted(factors, pieces[j], rows)
            total = [x + y for x, y in zip(total, term, strict=True)]
        step = rows // len(total)
        for i, part in enumerate(total):
            outs[k][i * step : (i + 1) * step, :] = part.astype(outs[k].dtype)


def state_call(body, mine, arrays, blocks, outs, heads, depth):
    fixed = lambda block: pl.BlockSpec(block[0], lambda i, s: block[1])
    return pl.pallas_call(
        body,
        out_shape=outs,
        grid_spec=pltpu.PrefetchScalarGridSpec(
            num_scalar_prefetch=1,
            grid=(1,),
            in_specs=[fixed(block) for block in blocks],
            out_specs=[fixed((out.shape, (0, 0))) for out in outs],
            scratch_shapes=[pltpu.VMEM((heads, depth), jnp.float32)],
        ),
        cost_estimate=pl.CostEstimate(
            flops=2**21, bytes_accessed=2**21, transcendentals=2**12
        ),
    )(mine, *arrays)


def plane_pairs(n_ctx, plane, k):
    return [(i, i // plane * plane + (i % plane ^ k)) for i in range(n_ctx)]


def up_pairs(n_ctx, plane, r):
    return [(i, i + r * plane) for i in range(n_ctx) if i + r * plane < n_ctx]


class Exchange:
    def __init__(self, dims, rows, heads, depth):
        self.dims, self.rows, self.heads, self.depth = dims, rows, heads, depth
        self.plane = dims[1] * dims[2]
        self.n_ctx = dims[0] * self.plane
        self.mine = lax.rem(lax.axis_index("ctx"), self.plane).astype(jnp.int32)
        self.place = self.mine.reshape(1)
        self.whole = ((rows, depth), (0, 0))
        self.tail = ((heads, depth), (rows // heads, 0))

    def send_in(self, pieces):
        got = []
        for k in range(self.plane):
            piece = lax.dynamic_index_in_dim(pieces, self.mine ^ k, 0, False)
            if k:
                piece = lax.ppermute(piece, "ctx", plane_pairs(self.n_ctx, self.plane, k))
            got.append(piece)
        return got

    def totals(self, got, tailed):
        own_tails = got is tailed
        size = self.rows + (self.heads if own_tails else 0)
        out = jax.ShapeDtypeStruct((size, self.depth), got[0].dtype)
        return state_call(
            functools.partial(mid_body, self.plane, self.rows, own_tails),
            self.place,
            [*got, *tailed],
            [self.whole] * self.plane + [self.tail] * self.plane,
            [out],
            self.heads,
            self.depth,
        )[0]

    def send_up(self, up):
        came = []
        for r in range(1, self.dims[0]):
            came.append(lax.ppermute(up, "ctx", up_pairs(self.n_ctx, self.plane, r)))
        return came

    def priors(self, got, tailed, came, came_tailed):
        shifts = self.dims[0] - 1
        out = jax.ShapeDtypeStruct((self.rows, self.depth), got[0].dtype)
        return state_call(
            functools.partial(post_body, self.plane, shifts, self.rows),
            self.place,
            [*got, *tailed, *came, *came_tailed],
            [self.whole] * self.plane
            + [self.tail] * self.plane
            + [self.whole] * shifts
            + [self.tail] * shifts,
            [out] * self.plane,
            self.heads,
            self.depth,
        )

    def send_out(self, priors):
        result = [priors[0]]
        for k in range(1, self.plane):
            result.append(lax.ppermute(priors[k], "ctx", plane_pairs(self.n_ctx, self.plane, k)))
        return result


def causal(cumul):
    length = cumul.shape[1]
    at = lax.broadcasted_iota(jnp.int32, (length, length), 0)
    of = lax.broadcasted_iota(jnp.int32, (length, length), 1)
    gap = down_rows(cumul, length) - jnp.broadcast_to(cumul, (length, length))
    return jnp.where(at >= of, jnp.exp(jnp.where(at >= of, gap, 0.0)), 0.0)


def prior_of(head, piece_refs, mine, depth):
    rows = piece_refs[0].shape[0]
    chunk = min(rows, depth)
    parts = []
    for start in range(0, depth, chunk):
        first = head * depth + start
        piece = first // rows
        at = pl.multiple_of(first % rows, chunk)
        part = jnp.zeros((chunk, depth), jnp.float32)
        for k, ref in enumerate(piece_refs):
            part = jnp.where((piece ^ mine) == k, ref[pl.ds(at, chunk), :].astype(jnp.float32), part)
        parts.append(part)
    return parts[0] if len(parts) == 1 else jnp.concatenate(parts, axis=0)


def solve_body(per_step, mine_ref, query_ref, unit_ref, cumul_ref, ridge_ref, *refs):
    pieces, answer_ref = refs[:-1], refs[-1]
    mine = mine_ref[0]
    length, depth = query_ref.shape[1:]
    spans = range(per_step)
    heads = [pl.program_id(0) * per_step + i for i in spans]
    units = [unit_ref[i] for i in spans]
    shares = [causal(cumul_ref[i]) for i in spans]
    starts = [jnp.exp(down_rows(cumul_ref[i], depth)) for i in spans]
    grams = [two_terms(prior_of(h, pieces, mine, depth)) for h in heads]
    remain = [unit_rows(query_ref[i]) for i in spans]
    direction = list(remain)
    answer = [jnp.zeros((length, depth), jnp.float32) for _ in spans]
    norm_now = [jnp.sum(r * r, axis=-1, keepdims=True) for r in remain]
    for _ in range(CG_STEPS):
        for i in spans:
            high, low = two_terms(direction[i])
            scores = (mm(high, units[i], 1, 1) + mm(low, units[i], 1, 1)) * shares[i]
            g_high, g_low = grams[i]
            prior = mm(high, g_high, 1, 1) + mm(low, g_high, 1, 1) + mm(high, g_low, 1, 1)
            applied = (
                starts[i] * prior
                + mm_split(scores, units[i], 1, 0)
                + ridge_ref[i] * direction[i]
            )
            length_of = norm_now[i] / jnp.sum(direction[i] * applied, axis=-1, keepdims=True)
            answer[i] = answer[i] + length_of * direction[i]
            remain[i] = remain[i] - length_of * applied
            norm_next = jnp.sum(remain[i] * remain[i], axis=-1, keepdims=True)
            direction[i] = remain[i] + (norm_next / norm_now[i]) * direction[i]
            norm_now[i] = norm_next
    for i in spans:
        answer_ref[i] = answer[i]


def read_body(per_step, mine_ref, answer_ref, unit_ref, value_ref, cumul_ref, *refs):
    pieces, out_ref = refs[:-1], refs[-1]
    mine = mine_ref[0]
    depth = answer_ref.shape[2]
    for i in range(per_step):
        head = pl.program_id(0) * per_step + i
        high, low = two_terms(answer_ref[i])
        held = prior_of(head, pieces, mine, depth).astype(jnp.bfloat16)
        start = jnp.exp(down_rows(cumul_ref[i], depth))
        prior = start * (mm(high, held, 1, 1) + mm(low, held, 1, 1))
        scores = (mm(high, unit_ref[i], 1, 1) + mm(low, unit_ref[i], 1, 1)) * causal(cumul_ref[i])
        out = prior + mm_split(scores, value_ref[i], 1, 0)
        out_ref[:, i * depth : (i + 1) * depth] = out.astype(jnp.bfloat16)


def head_call(body, mine, arrays, pieces, out, per_step, flops):
    heads, length, depth = arrays[0].shape
    by_head = lambda a: pl.BlockSpec((per_step, *a.shape[1:]), lambda i, s: (i, 0, 0))
    if len(out.shape) == 3:
        out_spec = by_head(out)
    else:
        out_spec = pl.BlockSpec((length, per_step * depth), lambda i, s: (0, i))
    return pl.pallas_call(
        functools.partial(body, per_step),
        out_shape=out,
        grid_spec=pltpu.PrefetchScalarGridSpec(
            num_scalar_prefetch=1,
            grid=(heads // per_step,),
            in_specs=[by_head(a) for a in arrays]
            + [pl.BlockSpec(p.shape, lambda i, s: (0, 0)) for p in pieces],
            out_specs=out_spec,
        ),
        cost_estimate=pl.CostEstimate(
            flops=flops, bytes_accessed=12 * heads * length * depth, transcendentals=heads * length * length
        ),
    )(mine, *arrays, *pieces)


def on_device(
    queries,
    key_vecs,
    values,
    log_decay,
    ridge_diag,
    residual,
    w_out,
    norm_gain,
    routes,
    gate_probs,
    w_gate,
    w_up,
    w_down,
):
    tok_dev, heads_dev, head_dim = queries.shape
    n_ctx = lax.axis_size("ctx")
    n_head = lax.axis_size("head")
    dims = grid_dims(n_ctx)
    core = lax.axis_index("head")
    swap = [(i, i ^ 1) for i in range(n_head)]

    tok_moe, top_count = routes.shape
    per_dev = w_gate.shape[0]
    expert_total = per_dev * n_ctx * n_head
    cap = 2 * tok_moe * top_count // expert_total
    own = (w_gate, w_up, w_down)
    other = tuple(lax.ppermute(w, "head", swap) for w in own)
    named = routes[:, :, None] == jnp.arange(expert_total, dtype=jnp.int32)[None, None, :]
    dense = jnp.sum(jnp.where(named, gate_probs[:, :, None], 0.0), axis=1)
    table = dense.T.reshape(n_ctx, n_head * per_dev, tok_moe)
    keys_h = key_vecs.transpose(1, 0, 2)
    values_h = values.transpose(1, 0, 2)
    queries_h = queries.transpose(1, 0, 2)
    cumul_log = jnp.cumsum(log_decay, axis=1)
    cumul_h = cumul_log[:, None, :]
    plane = dims[1] * dims[2]
    unit_h, gram_pieces, held_pieces = prep(keys_h, values_h, cumul_log, plane)
    swap_state = Exchange(dims, heads_dev * head_dim // plane, heads_dev, head_dim)
    gram_got = swap_state.send_in(gram_pieces)
    held_got = swap_state.send_in(held_pieces)
    gram_up = swap_state.totals(gram_got, gram_got)
    gram_up, table = lax.optimization_barrier((gram_up, table))
    gram_came = swap_state.send_up(gram_up)
    held_up = swap_state.totals(held_got, gram_got)
    held_came = swap_state.send_up(held_up)
    gate_of = lax.all_to_all(table, "ctx", split_axis=0, concat_axis=0, tiled=True)
    gram_prior = swap_state.priors(gram_got, gram_got, gram_came, gram_came)
    gram_prior = swap_state.send_out(gram_prior)
    held_prior = swap_state.priors(held_got, gram_got, held_came, gram_came)
    held_prior = swap_state.send_out(held_prior)
    gram_prior, gate_of = lax.optimization_barrier((gram_prior, gate_of))
    split = gate_of.reshape(n_ctx, n_head, per_dev, tok_moe)
    gate_of = jnp.where(core == 0, split, split[:, ::-1]).reshape(gate_of.shape)
    routed = (gate_of != 0.0).astype(jnp.bfloat16)
    earlier = (jnp.arange(tok_moe)[:, None] < jnp.arange(tok_moe)[None, :]).astype(jnp.bfloat16)
    before = jnp.einsum("set,tu->seu", routed, earlier, preferred_element_type=jnp.float32)
    slot_of = jnp.where(gate_of != 0.0, before.astype(jnp.int32), -1)

    per_step = 2 if heads_dev % 2 == 0 else 1
    work = heads_dev * tok_dev * head_dim
    answer = head_call(
        solve_body,
        swap_state.place,
        [queries_h, unit_h, cumul_h, ridge_diag[:, None, :]],
        gram_prior,
        jax.ShapeDtypeStruct(queries_h.shape, jnp.float32),
        per_step,
        CG_STEPS * work * (8 * tok_dev + 6 * head_dim),
    )
    mesa_rows = head_call(
        read_body,
        swap_state.place,
        [answer, unit_h, values_h, cumul_h],
        held_prior,
        jax.ShapeDtypeStruct((tok_dev, heads_dev * head_dim), jnp.bfloat16),
        per_step,
        work * (8 * tok_dev + 4 * head_dim),
    )
    here = lax.dynamic_slice_in_dim(mesa_rows, core * tok_moe, tok_moe, 0)
    there = lax.dynamic_slice_in_dim(mesa_rows, (1 - core) * tok_moe, tok_moe, 0)
    sent = jnp.dot(there, w_out, preferred_element_type=jnp.float32).astype(jnp.bfloat16)
    came = lax.ppermute(sent, "head", swap)
    kept = jnp.dot(here, w_out, preferred_element_type=jnp.float32)
    attended = (residual.astype(jnp.float32) + kept + came.astype(jnp.float32)).astype(jnp.bfloat16)
    att_f = attended.astype(jnp.float32)
    normed = (
        att_f * lax.rsqrt(jnp.mean(att_f * att_f, axis=-1, keepdims=True) + norm_eps) * norm_gain
    ).astype(jnp.bfloat16)

    groups = spread(normed, dims, n_head)
    back = []
    for r0 in call_order(dims[0]):
        group = groups[r0]
        sources = [
            slot_source((r0, ra, rb), dims) for rb in range(len(group)) for ra in range(len(group[0]))
        ]
        sources = lax.optimization_barrier(jnp.stack(sources))
        outs = run_experts(group, sources, slot_of, gate_of, own, other, cap)
        back.append(collect(outs, r0, dims, n_head))
    layer_out = add_all(att_f, back, jnp.bfloat16)
    return (attended, layer_out)


def solution(mesh):
    in_specs = (
        P("ctx", "head", None),
        P("ctx", "head", None),
        P("ctx", "head", None),
        P("head", "ctx"),
        P("head", None),
        P(("ctx", "head"), None),
        P("head", None),
        P(),
        P(("ctx", "head"), None),
        P(("ctx", "head"), None),
        P(("ctx", "head"), None, None),
        P(("ctx", "head"), None, None),
        P(("ctx", "head"), None, None),
    )
    out_specs = (P(("ctx", "head"), None), P(("ctx", "head"), None))

    return jax.shard_map(
        on_device, mesh=mesh, in_specs=in_specs, out_specs=out_specs, check_vma=False
    )
```

```python
import functools

import jax
import jax.numpy as jnp
from jax import lax
from jax.experimental import pallas as pl
from jax.experimental.pallas import tpu as pltpu
from jax.sharding import PartitionSpec as P

CG_STEPS = 4

norm_eps = 1e-06
BOTH = ("ctx", "head")


def grid_dims(count):
    bits = count.bit_length() - 1
    if 1 << bits != count:
        return (count, 1, 1)
    first = -(-bits // 3)
    second = -(-(bits - first) // 2)
    return (1 << first, 1 << second, 1 << (bits - first - second))


def shifted(place, dims, dim, by):
    coords = [place // (dims[1] * dims[2]), place // dims[2] % dims[1], place % dims[2]]
    coords[dim] = (coords[dim] + by) % dims[dim]
    return (coords[0] * dims[1] + coords[1]) * dims[2] + coords[2]


def phase_dims(dims):
    if dims[1] == dims[2]:
        return ((0, 2, 1), (0, 1, 2))
    return ((0, 2, 1), (0, 2, 1))


def hop(block, dims, n_head, phase, by):
    orders = phase_dims(dims)
    count = dims[0] * dims[1] * dims[2]
    pairs = []
    for place in range(count):
        for core in range(n_head):
            dest = shifted(place, dims, orders[core % 2][phase], by)
            pairs.append((place * n_head + core, dest * n_head + core))
    return lax.ppermute(block, BOTH, pairs)


def slot_sizes(dims):
    order = phase_dims(dims)[0]
    return tuple(dims[d] for d in order)


def spread(block, dims, n_head):
    s0, sa, sb = slot_sizes(dims)
    heads = [block]
    for r0 in visit(s0)[1:]:
        heads.append(hop(block, dims, n_head, 0, r0))
    groups = {}
    for r0, head in zip(visit(s0), heads, strict=True):
        line = [head]
        for ra in range(1, sa):
            line.append(hop(head, dims, n_head, 1, ra))
        group = [line]
        for rb in range(1, sb):
            group.append([hop(one, dims, n_head, 2, rb) for one in line])
        groups[r0] = group
    return groups


def visit(size):
    return [0] + sorted(range(1, size), key=lambda r: (-min(r, size - r), r))


def add_all(first, others, dtype):
    total = first.astype(jnp.float32)
    for other in others:
        total = total + other.astype(jnp.float32)
    return total.astype(dtype)


def collect(outs, r0, dims, n_head):
    _, sa, sb = slot_sizes(dims)
    rows = outs[0].shape[0] // sa
    came = []
    for rb in range(1, sb):
        came.append(hop(outs[rb], dims, n_head, 2, -rb))
    part = lambda array, ra: array[ra * rows : (ra + 1) * rows]
    line = []
    for ra in range(1, sa):
        total = add_all(part(outs[0], ra), [part(c, ra) for c in came], jnp.bfloat16)
        line.append(hop(total, dims, n_head, 1, -ra))
    total = add_all(part(outs[0], 0), [part(c, 0) for c in came] + line, jnp.bfloat16)
    if r0 == 0:
        return total
    return hop(total, dims, n_head, 0, -r0)


def slot_source(key, dims):
    place = lax.axis_index("ctx")
    core = lax.axis_index("head") % 2
    orders = phase_dims(dims)
    sources = []
    for order in orders:
        coords = [place // (dims[1] * dims[2]), place // dims[2] % dims[1], place % dims[2]]
        for dim, by in zip(order, key, strict=True):
            coords[dim] = (coords[dim] - by) % dims[dim]
        sources.append((coords[0] * dims[1] + coords[1]) * dims[2] + coords[2])
    return jnp.where(core == 0, sources[0], sources[1]).astype(jnp.int32)


def expert_body(n_a, n_b, n_expert, cap, n_tiles, src_ref, slot_ref, gate_ref, *refs):
    n_blocks = n_a * n_b
    blocks = refs[:n_blocks]
    gate_own, up_own, down_own, gate_oth, up_oth, down_oth = refs[n_blocks : n_blocks + 6]
    outs = refs[n_blocks + 6 : n_blocks + 6 + n_b]
    picked, hidden_of, scaled, select = refs[n_blocks + 6 + n_b :]
    expert = pl.program_id(0)
    tile = pl.program_id(1)
    tokens = blocks[0].shape[0]

    @pl.when((expert == 0) & (tile == 0))
    def _():
        for b in range(n_blocks):
            src = src_ref[b]
            for e in range(n_expert):
                wanted = slot_ref[src, pl.ds(e, 1), :]
                at = lax.broadcasted_iota(jnp.int32, (cap, tokens), 0)
                hit = (at == jnp.broadcast_to(wanted, (cap, tokens))).astype(jnp.float32)
                select[b, pl.ds(e * cap, cap), :] = hit.astype(jnp.bfloat16)
            got = jnp.dot(select[b], blocks[b][...], preferred_element_type=jnp.float32).astype(
                jnp.bfloat16
            )
            for e in range(n_expert):
                picked[e, pl.ds(b * cap, cap), :] = got[e * cap : (e + 1) * cap]

    def step(w_gate, w_up):
        tokens_in = picked[expert]
        gate_h = jnp.dot(tokens_in, w_gate[0], preferred_element_type=jnp.float32)
        up_h = jnp.dot(tokens_in, w_up[0], preferred_element_type=jnp.float32)
        hidden = gate_h * (1.0 / (1.0 + jnp.exp(-gate_h))) * up_h
        hidden_of[tile] = hidden.astype(jnp.bfloat16)

    def finish(w_down):
        hidden = jnp.concatenate([hidden_of[i] for i in range(n_tiles)], axis=1)
        result = jnp.dot(hidden, w_down[0], preferred_element_type=jnp.float32)
        for b in range(n_blocks):
            src = src_ref[b]
            weight_row = gate_ref[src, pl.ds(expert, 1), :]
            hit = select[b, pl.ds(expert * cap, cap), :].astype(jnp.float32)
            weight = jnp.sum(hit * weight_row, axis=1, keepdims=True)
            scaled[b, pl.ds(expert * cap, cap), :] = (
                result[b * cap : (b + 1) * cap] * weight
            ).astype(jnp.bfloat16)

    @pl.when(expert < n_expert // 2)
    def _():
        step(gate_own, up_own)

        @pl.when(tile == n_tiles - 1)
        def _():
            finish(down_own)

    @pl.when(expert >= n_expert // 2)
    def _():
        step(gate_oth, up_oth)

        @pl.when(tile == n_tiles - 1)
        def _():
            finish(down_oth)

    @pl.when((tile == n_tiles - 1) & (expert == n_expert - 1))
    def _():
        for b in range(n_blocks):
            back = jnp.transpose(select[b].astype(jnp.float32)).astype(jnp.bfloat16)
            outs[b // n_a][pl.ds(b % n_a * tokens, tokens), :] = jnp.dot(
                back, scaled[b], preferred_element_type=jnp.float32
            ).astype(jnp.bfloat16)


def run_experts(group, sources, slot_of, gate_of, own, other, cap):
    n_b, n_a = len(group), len(group[0])
    blocks = [block for line in group for block in line]
    n_blocks = len(blocks)
    tokens, width = blocks[0].shape
    per_dev, _, hidden = own[0].shape
    n_expert = 2 * per_dev
    tile_f = 256 if hidden % 256 == 0 else hidden
    n_tiles = hidden // tile_f
    last = n_tiles - 1
    whole = lambda shape: pl.BlockSpec(
        shape, lambda e, f, s: (0,) * len(shape), pipeline_mode=pl.Buffered(1)
    )

    def own_at(e, f):
        here = e < per_dev
        return jnp.where(here, e, per_dev - 1), jnp.where(here, f, last)

    def other_at(e, f):
        here = e >= per_dev
        return jnp.where(here, e - per_dev, 0), jnp.where(here, f, 0)

    def in_spec(at):
        return pl.BlockSpec((1, width, tile_f), lambda e, f, s: (at(e, f)[0], 0, at(e, f)[1]))

    def out_spec(at):
        return pl.BlockSpec((1, hidden, width), lambda e, f, s: (at(e, f)[0], 0, 0))

    rows = n_blocks * cap
    flops = 2 * n_expert * rows * width * hidden * 3
    moved = 2 * (2 * n_blocks * tokens * width + n_expert * 3 * width * hidden)
    return pl.pallas_call(
        functools.partial(expert_body, n_a, n_b, n_expert, cap, n_tiles),
        out_shape=[jax.ShapeDtypeStruct((n_a * tokens, width), jnp.bfloat16)] * n_b,
        grid_spec=pltpu.PrefetchScalarGridSpec(
            num_scalar_prefetch=1,
            grid=(n_expert, n_tiles),
            in_specs=[whole(slot_of.shape), whole(gate_of.shape)]
            + [whole((tokens, width))] * n_blocks
            + [in_spec(own_at), in_spec(own_at), out_spec(own_at)]
            + [in_spec(other_at), in_spec(other_at), out_spec(other_at)],
            out_specs=[whole((n_a * tokens, width))] * n_b,
            scratch_shapes=[
                pltpu.VMEM((n_expert, rows, width), jnp.bfloat16),
                pltpu.VMEM((n_tiles, rows, tile_f), jnp.bfloat16),
                pltpu.VMEM((n_blocks, n_expert * cap, width), jnp.bfloat16),
                pltpu.VMEM((n_blocks, n_expert * cap, tokens), jnp.bfloat16),
            ],
        ),
        compiler_params=pltpu.CompilerParams(
            dimension_semantics=("arbitrary", "arbitrary"), vmem_limit_bytes=60 * 1024 * 1024
        ),
        cost_estimate=pl.CostEstimate(
            flops=flops, bytes_accessed=moved, transcendentals=n_expert * rows * hidden
        ),
    )(sources, slot_of, gate_of, *blocks, *own, *other)


def two_terms(exact):
    high = exact.astype(jnp.bfloat16)
    return high, (exact - high.astype(jnp.float32)).astype(jnp.bfloat16)


def mm(lhs, rhs, at_lhs, at_rhs):
    return lax.dot_general(
        lhs, rhs, (((at_lhs,), (at_rhs,)), ((), ())), preferred_element_type=jnp.float32
    )


def mm_split(exact, narrow, at_lhs, at_rhs):
    high, low = two_terms(exact)
    return mm(high, narrow, at_lhs, at_rhs) + mm(low, narrow, at_lhs, at_rhs)


def unit_rows(vectors):
    floats = vectors.astype(jnp.float32)
    return floats * lax.rsqrt(jnp.sum(floats * floats, axis=-1, keepdims=True) + norm_eps)


def down_rows(row, lanes):
    return jnp.transpose(jnp.broadcast_to(row, (lanes, row.shape[1])))


def prep_body(rows, mine_ref, key_ref, value_ref, cumul_ref, unit_ref, *refs):
    heads, length, depth = key_ref.shape
    plane = heads * depth // rows
    gram_refs, held_refs = refs[:plane], refs[plane : 2 * plane]
    gram_all, held_all = refs[2 * plane :]
    last = cumul_ref[:, length - 1 : length]
    chunk = min(rows, depth)
    for h in range(heads):
        unit = unit_rows(key_ref[h]).astype(jnp.bfloat16)
        unit_ref[h] = unit
        left = last[h : h + 1] - cumul_ref[h : h + 1, :]
        faded = unit.astype(jnp.float32) * jnp.exp(down_rows(left, depth))
        high, low = two_terms(faded)
        gram = mm(high, unit, 0, 0) + mm(low, unit, 0, 0)
        held = mm(value_ref[h], high, 0, 0) + mm(value_ref[h], low, 0, 0)
        for start in range(0, depth, chunk):
            piece, at = divmod(h * depth + start, rows)
            gram_all[piece, at : at + chunk, :] = gram[start : start + chunk]
            held_all[piece, at : at + chunk, :] = held[start : start + chunk]
    tails = jnp.broadcast_to(last, (heads, depth))
    for k in range(plane):
        piece = mine_ref[0] ^ k
        gram_refs[k][0:rows, :] = gram_all[piece]
        gram_refs[k][rows : rows + heads, :] = tails
        held_refs[k][...] = held_all[piece].astype(jnp.bfloat16)


def prep(place, keys, values, cumul_log, plane):
    heads, length, depth = keys.shape
    rows = heads * depth // plane
    outs = (
        [jax.ShapeDtypeStruct(keys.shape, jnp.bfloat16)]
        + [jax.ShapeDtypeStruct((rows + heads, depth), jnp.float32)] * plane
        + [jax.ShapeDtypeStruct((rows, depth), jnp.bfloat16)] * plane
    )
    whole = lambda a: pl.BlockSpec(a.shape, lambda i, s: (0,) * len(a.shape))
    unit, *pieces = pl.pallas_call(
        functools.partial(prep_body, rows),
        out_shape=outs,
        grid_spec=pltpu.PrefetchScalarGridSpec(
            num_scalar_prefetch=1,
            grid=(1,),
            in_specs=[whole(keys), whole(values), whole(cumul_log)],
            out_specs=[whole(out) for out in outs],
            scratch_shapes=[pltpu.VMEM((plane, rows, depth), jnp.float32)] * 2,
        ),
        cost_estimate=pl.CostEstimate(
            flops=8 * heads * length * depth * depth,
            bytes_accessed=8 * heads * length * depth,
            transcendentals=heads * length * depth,
        ),
        name="prep",
    )(place, keys, values, cumul_log)
    return unit, pieces[:plane], pieces[plane:]


def plane_sums(tails, mine):
    count = len(tails)
    upto, before = [], []
    for k in range(count):
        total = jnp.zeros_like(tails[0])
        for j in range(count):
            total = total + jnp.where((mine ^ j) < (mine ^ k), tails[j], 0.0)
        before.append(total)
        upto.append(total + tails[k])
    return upto, before, functools.reduce(lambda x, y: x + y, tails)


def by_row(factors, table_ref, mine, rows, depth):
    table_ref[...] = factors
    span = max(1, rows // depth)
    first = mine * rows // depth
    return [table_ref[pl.ds(first + i, 1), :] for i in range(span)]


def weighted(factors, piece_ref, rows):
    step = rows // len(factors)
    return [
        f * piece_ref[i * step : (i + 1) * step, :].astype(jnp.float32)
        for i, f in enumerate(factors)
    ]


def mid_body(count, rows, tailed, mine_ref, *refs):
    pieces, tail_refs, up_ref, table_ref = refs[:count], refs[count : -2], refs[-2], refs[-1]
    heads, depth = table_ref.shape
    mine = mine_ref[0]
    tails = [t[...] for t in tail_refs]
    upto, _, every = plane_sums(tails, mine)
    total = None
    for k in range(count):
        factors = by_row(jnp.exp(every - upto[k]), table_ref, mine, rows, depth)
        term = weighted(factors, pieces[k], rows)
        total = term if total is None else [x + y for x, y in zip(total, term, strict=True)]
    step = rows // len(total)
    for i, part in enumerate(total):
        up_ref[i * step : (i + 1) * step, :] = part.astype(up_ref.dtype)
    if tailed:
        up_ref[rows : rows + heads, :] = every


def post_body(count, shifts, rows, mine_ref, *refs):
    pieces, tail_refs = refs[:count], refs[count : 2 * count]
    came = refs[2 * count : 2 * count + shifts]
    came_tails = refs[2 * count + shifts : 2 * count + 2 * shifts]
    outs, table_ref = refs[2 * count + 2 * shifts : -1], refs[-1]
    heads, depth = table_ref.shape
    mine = mine_ref[0]
    upto, before, _ = plane_sums([t[...] for t in tail_refs], mine)
    lost = jnp.zeros((heads, depth), jnp.float32)
    below = None
    for r in range(shifts):
        factors = by_row(jnp.exp(lost), table_ref, mine, rows, depth)
        term = weighted(factors, came[r], rows)
        below = term if below is None else [x + y for x, y in zip(below, term, strict=True)]
        lost = lost + came_tails[r][...]
    for k in range(count):
        factors = by_row(jnp.exp(before[k]), table_ref, mine, rows, depth)
        if below is None:
            total = [jnp.zeros((rows // len(factors), depth), jnp.float32)] * len(factors)
        else:
            total = [f * part for f, part in zip(factors, below, strict=True)]
        for j in range(count):
            if j == k:
                continue
            earlier = (mine ^ j) < (mine ^ k)
            share = jnp.where(earlier, jnp.exp(jnp.where(earlier, before[k] - upto[j], 0.0)), 0.0)
            factors = by_row(share, table_ref, mine, rows, depth)
            term = weighted(factors, pieces[j], rows)
            total = [x + y for x, y in zip(total, term, strict=True)]
        step = rows // len(total)
        for i, part in enumerate(total):
            outs[k][i * step : (i + 1) * step, :] = part.astype(outs[k].dtype)


def state_call(body, mine, arrays, blocks, outs, heads, depth):
    fixed = lambda block: pl.BlockSpec(block[0], lambda i, s: block[1])
    return pl.pallas_call(
        body,
        out_shape=outs,
        grid_spec=pltpu.PrefetchScalarGridSpec(
            num_scalar_prefetch=1,
            grid=(1,),
            in_specs=[fixed(block) for block in blocks],
            out_specs=[fixed((out.shape, (0, 0))) for out in outs],
            scratch_shapes=[pltpu.VMEM((heads, depth), jnp.float32)],
        ),
        cost_estimate=pl.CostEstimate(
            flops=2**21, bytes_accessed=2**21, transcendentals=2**12
        ),
    )(mine, *arrays)


def plane_pairs(n_ctx, plane, k):
    return [(i, i // plane * plane + (i % plane ^ k)) for i in range(n_ctx)]


def up_pairs(n_ctx, plane, r):
    return [(i, i + r * plane) for i in range(n_ctx) if i + r * plane < n_ctx]


class Exchange:
    def __init__(self, dims, rows, heads, depth):
        self.dims, self.rows, self.heads, self.depth = dims, rows, heads, depth
        self.plane = dims[1] * dims[2]
        self.n_ctx = dims[0] * self.plane
        self.mine = lax.rem(lax.axis_index("ctx"), self.plane).astype(jnp.int32)
        self.place = self.mine.reshape(1)
        self.whole = ((rows, depth), (0, 0))
        self.tail = ((heads, depth), (rows // heads, 0))

    def send_in(self, pieces):
        got = []
        for k in range(self.plane):
            piece = pieces[k]
            if k:
                piece = lax.ppermute(piece, "ctx", plane_pairs(self.n_ctx, self.plane, k))
            got.append(piece)
        return got

    def totals(self, got, tailed):
        own_tails = got is tailed
        size = self.rows + (self.heads if own_tails else 0)
        out = jax.ShapeDtypeStruct((size, self.depth), got[0].dtype)
        return state_call(
            functools.partial(mid_body, self.plane, self.rows, own_tails),
            self.place,
            [*got, *tailed],
            [self.whole] * self.plane + [self.tail] * self.plane,
            [out],
            self.heads,
            self.depth,
        )[0]

    def send_up(self, up):
        came = []
        for r in range(1, self.dims[0]):
            came.append(lax.ppermute(up, "ctx", up_pairs(self.n_ctx, self.plane, r)))
        return came

    def priors(self, got, tailed, came, came_tailed):
        shifts = self.dims[0] - 1
        out = jax.ShapeDtypeStruct((self.rows, self.depth), got[0].dtype)
        return state_call(
            functools.partial(post_body, self.plane, shifts, self.rows),
            self.place,
            [*got, *tailed, *came, *came_tailed],
            [self.whole] * self.plane
            + [self.tail] * self.plane
            + [self.whole] * shifts
            + [self.tail] * shifts,
            [out] * self.plane,
            self.heads,
            self.depth,
        )

    def send_out(self, priors):
        result = [priors[0]]
        for k in range(1, self.plane):
            result.append(lax.ppermute(priors[k], "ctx", plane_pairs(self.n_ctx, self.plane, k)))
        return result


def causal(cumul):
    length = cumul.shape[1]
    at = lax.broadcasted_iota(jnp.int32, (length, length), 0)
    of = lax.broadcasted_iota(jnp.int32, (length, length), 1)
    gap = down_rows(cumul, length) - jnp.broadcast_to(cumul, (length, length))
    return jnp.where(at >= of, jnp.exp(jnp.where(at >= of, gap, 0.0)), 0.0)


def prior_of(head, piece_refs, mine, depth):
    rows = piece_refs[0].shape[0]
    chunk = min(rows, depth)
    parts = []
    for start in range(0, depth, chunk):
        first = head * depth + start
        piece = first // rows
        at = pl.multiple_of(first % rows, chunk)
        part = jnp.zeros((chunk, depth), jnp.float32)
        for k, ref in enumerate(piece_refs):
            part = jnp.where((piece ^ mine) == k, ref[pl.ds(at, chunk), :].astype(jnp.float32), part)
        parts.append(part)
    return parts[0] if len(parts) == 1 else jnp.concatenate(parts, axis=0)


def solve_body(per_step, mine_ref, query_ref, unit_ref, cumul_ref, ridge_ref, *refs):
    pieces, answer_ref = refs[:-1], refs[-1]
    mine = mine_ref[0]
    length, depth = query_ref.shape[1:]
    spans = range(per_step)
    heads = [pl.program_id(0) * per_step + i for i in spans]
    units = [unit_ref[i] for i in spans]
    shares = [causal(cumul_ref[i]) for i in spans]
    starts = [jnp.exp(down_rows(cumul_ref[i], depth)) for i in spans]
    grams = [two_terms(prior_of(h, pieces, mine, depth)) for h in heads]
    remain = [unit_rows(query_ref[i]) for i in spans]
    direction = list(remain)
    answer = [jnp.zeros((length, depth), jnp.float32) for _ in spans]
    norm_now = [jnp.sum(r * r, axis=-1, keepdims=True) for r in remain]
    for _ in range(CG_STEPS):
        for i in spans:
            high, low = two_terms(direction[i])
            scores = (mm(high, units[i], 1, 1) + mm(low, units[i], 1, 1)) * shares[i]
            g_high, g_low = grams[i]
            prior = mm(high, g_high, 1, 1) + mm(low, g_high, 1, 1) + mm(high, g_low, 1, 1)
            applied = (
                starts[i] * prior
                + mm_split(scores, units[i], 1, 0)
                + ridge_ref[i] * direction[i]
            )
            length_of = norm_now[i] / jnp.sum(direction[i] * applied, axis=-1, keepdims=True)
            answer[i] = answer[i] + length_of * direction[i]
            remain[i] = remain[i] - length_of * applied
            norm_next = jnp.sum(remain[i] * remain[i], axis=-1, keepdims=True)
            direction[i] = remain[i] + (norm_next / norm_now[i]) * direction[i]
            norm_now[i] = norm_next
    for i in spans:
        answer_ref[i] = answer[i]


def read_body(per_step, mine_ref, answer_ref, unit_ref, value_ref, cumul_ref, *refs):
    pieces, out_ref = refs[:-1], refs[-1]
    mine = mine_ref[0]
    depth = answer_ref.shape[2]
    for i in range(per_step):
        head = pl.program_id(0) * per_step + i
        high, low = two_terms(answer_ref[i])
        held = prior_of(head, pieces, mine, depth).astype(jnp.bfloat16)
        start = jnp.exp(down_rows(cumul_ref[i], depth))
        prior = start * (mm(high, held, 1, 1) + mm(low, held, 1, 1))
        scores = (mm(high, unit_ref[i], 1, 1) + mm(low, unit_ref[i], 1, 1)) * causal(cumul_ref[i])
        out = prior + mm_split(scores, value_ref[i], 1, 0)
        out_ref[:, i * depth : (i + 1) * depth] = out.astype(jnp.bfloat16)


def head_call(body, mine, arrays, pieces, out, per_step, flops):
    heads, length, depth = arrays[0].shape
    by_head = lambda a: pl.BlockSpec((per_step, *a.shape[1:]), lambda i, s: (i, 0, 0))
    if len(out.shape) == 3:
        out_spec = by_head(out)
    else:
        out_spec = pl.BlockSpec((length, per_step * depth), lambda i, s: (0, i))
    return pl.pallas_call(
        functools.partial(body, per_step),
        out_shape=out,
        grid_spec=pltpu.PrefetchScalarGridSpec(
            num_scalar_prefetch=1,
            grid=(heads // per_step,),
            in_specs=[by_head(a) for a in arrays]
            + [pl.BlockSpec(p.shape, lambda i, s: (0, 0)) for p in pieces],
            out_specs=out_spec,
        ),
        cost_estimate=pl.CostEstimate(
            flops=flops, bytes_accessed=12 * heads * length * depth, transcendentals=heads * length * length
        ),
    )(mine, *arrays, *pieces)


def on_device(
    queries,
    key_vecs,
    values,
    log_decay,
    ridge_diag,
    residual,
    w_out,
    norm_gain,
    routes,
    gate_probs,
    w_gate,
    w_up,
    w_down,
):
    tok_dev, heads_dev, head_dim = queries.shape
    n_ctx = lax.axis_size("ctx")
    n_head = lax.axis_size("head")
    dims = grid_dims(n_ctx)
    core = lax.axis_index("head")
    swap = [(i, i ^ 1) for i in range(n_head)]

    tok_moe, top_count = routes.shape
    per_dev = w_gate.shape[0]
    expert_total = per_dev * n_ctx * n_head
    cap = 2 * tok_moe * top_count // expert_total
    own = (w_gate, w_up, w_down)
    other = tuple(lax.ppermute(w, "head", swap) for w in own)
    named = routes[:, :, None] == jnp.arange(expert_total, dtype=jnp.int32)[None, None, :]
    dense = jnp.sum(jnp.where(named, gate_probs[:, :, None], 0.0), axis=1)
    table = dense.T.reshape(n_ctx, n_head * per_dev, tok_moe)
    keys_h = key_vecs.transpose(1, 0, 2)
    values_h = values.transpose(1, 0, 2)
    queries_h = queries.transpose(1, 0, 2)
    cumul_log = jnp.cumsum(log_decay, axis=1)
    cumul_h = cumul_log[:, None, :]
    plane = dims[1] * dims[2]
    swap_state = Exchange(dims, heads_dev * head_dim // plane, heads_dev, head_dim)
    unit_h, gram_pieces, held_pieces = prep(swap_state.place, keys_h, values_h, cumul_log, plane)
    gram_got = swap_state.send_in(gram_pieces)
    held_got = swap_state.send_in(held_pieces)
    gram_up = swap_state.totals(gram_got, gram_got)
    gram_came = swap_state.send_up(gram_up)
    held_up = swap_state.totals(held_got, gram_got)
    held_came = swap_state.send_up(held_up)
    gram_prior = swap_state.priors(gram_got, gram_got, gram_came, gram_came)
    gram_prior = swap_state.send_out(gram_prior)
    held_prior = swap_state.priors(held_got, gram_got, held_came, gram_came)
    held_prior = swap_state.send_out(held_prior)
    per_step = 4 if heads_dev % 4 == 0 else 1
    work = heads_dev * tok_dev * head_dim
    answer = head_call(
        solve_body,
        swap_state.place,
        [queries_h, unit_h, cumul_h, ridge_diag[:, None, :]],
        gram_prior,
        jax.ShapeDtypeStruct(queries_h.shape, jnp.float32),
        per_step,
        CG_STEPS * work * (8 * tok_dev + 6 * head_dim),
    )
    mesa_rows = head_call(
        read_body,
        swap_state.place,
        [answer, unit_h, values_h, cumul_h],
        held_prior,
        jax.ShapeDtypeStruct((tok_dev, heads_dev * head_dim), jnp.bfloat16),
        per_step,
        work * (8 * tok_dev + 4 * head_dim),
    )
    partial = jnp.dot(mesa_rows, w_out, preferred_element_type=jnp.float32)
    sent = lax.dynamic_slice_in_dim(partial, (1 - core) * tok_moe, tok_moe, 0)
    came = lax.ppermute(sent.astype(jnp.bfloat16), "head", swap)
    kept = lax.dynamic_slice_in_dim(partial, core * tok_moe, tok_moe, 0)
    attended = (residual.astype(jnp.float32) + kept + came.astype(jnp.float32)).astype(jnp.bfloat16)
    att_f = attended.astype(jnp.float32)
    normed = (
        att_f * lax.rsqrt(jnp.mean(att_f * att_f, axis=-1, keepdims=True) + norm_eps) * norm_gain
    ).astype(jnp.bfloat16)

    groups = spread(normed, dims, n_head)
    gate_of = lax.all_to_all(table, "ctx", split_axis=0, concat_axis=0, tiled=True)
    split = gate_of.reshape(n_ctx, n_head, per_dev, tok_moe)
    gate_of = jnp.where(core == 0, split, split[:, ::-1]).reshape(gate_of.shape)
    routed = (gate_of != 0.0).astype(jnp.bfloat16)
    earlier = (jnp.arange(tok_moe)[:, None] < jnp.arange(tok_moe)[None, :]).astype(jnp.bfloat16)
    before = jnp.einsum("set,tu->seu", routed, earlier, preferred_element_type=jnp.float32)
    slot_of = jnp.where(gate_of != 0.0, before.astype(jnp.int32), -1)

    back = []
    for r0, group in groups.items():
        sources = [
            slot_source((r0, ra, rb), dims) for rb in range(len(group)) for ra in range(len(group[0]))
        ]
        sources = lax.optimization_barrier(jnp.stack(sources))
        outs = run_experts(group, sources, slot_of, gate_of, own, other, cap)
        back.append(collect(outs, r0, dims, n_head))
    layer_out = add_all(att_f, back, jnp.bfloat16)
    return (attended, layer_out)


def solution(mesh):
    in_specs = (
        P("ctx", "head", None),
        P("ctx", "head", None),
        P("ctx", "head", None),
        P("head", "ctx"),
        P("head", None),
        P(("ctx", "head"), None),
        P("head", None),
        P(),
        P(("ctx", "head"), None),
        P(("ctx", "head"), None),
        P(("ctx", "head"), None, None),
        P(("ctx", "head"), None, None),
        P(("ctx", "head"), None, None),
    )
    out_specs = (P(("ctx", "head"), None), P(("ctx", "head"), None))

    return jax.shard_map(
        on_device, mesh=mesh, in_specs=in_specs, out_specs=out_specs, check_vma=False
    )
```

```python
import functools

import jax
import jax.numpy as jnp
from jax import lax
from jax.experimental import pallas as pl
from jax.experimental.pallas import tpu as pltpu
from jax.sharding import PartitionSpec as P

CG_STEPS = 4

norm_eps = 1e-06
BOTH = ("ctx", "head")


def grid_dims(count):
    bits = count.bit_length() - 1
    if 1 << bits != count:
        return (count, 1, 1)
    first = -(-bits // 3)
    second = -(-(bits - first) // 2)
    return (1 << first, 1 << second, 1 << (bits - first - second))


def shifted(place, dims, dim, by):
    coords = [place // (dims[1] * dims[2]), place // dims[2] % dims[1], place % dims[2]]
    coords[dim] = (coords[dim] + by) % dims[dim]
    return (coords[0] * dims[1] + coords[1]) * dims[2] + coords[2]


def phase_dims(dims):
    if dims[1] == dims[2]:
        return ((0, 2, 1), (0, 1, 2))
    return ((0, 2, 1), (0, 2, 1))


def hop(block, dims, n_head, phase, by):
    orders = phase_dims(dims)
    count = dims[0] * dims[1] * dims[2]
    pairs = []
    for place in range(count):
        for core in range(n_head):
            dest = shifted(place, dims, orders[core % 2][phase], by)
            pairs.append((place * n_head + core, dest * n_head + core))
    return lax.ppermute(block, BOTH, pairs)


def slot_sizes(dims):
    order = phase_dims(dims)[0]
    return tuple(dims[d] for d in order)


def spread(block, dims, n_head):
    s0, sa, sb = slot_sizes(dims)
    heads = [block]
    for r0 in visit(s0)[1:]:
        heads.append(hop(block, dims, n_head, 0, r0))
    groups = {}
    for r0, head in zip(visit(s0), heads, strict=True):
        line = [head]
        for ra in range(1, sa):
            line.append(hop(head, dims, n_head, 1, ra))
        group = [line]
        for rb in range(1, sb):
            sent = [hop(head, dims, n_head, 2, rb)]
            sent += [hop(one, dims, n_head, 2, rb) for one in line[1:]]
            group.append(sent)
        groups[r0] = group
    return groups


def visit(size):
    return list(range(size))


def add_all(first, others, dtype):
    total = first.astype(jnp.float32)
    for other in others:
        total = total + other.astype(jnp.float32)
    return total.astype(dtype)


def collect(outs, r0, dims, n_head):
    _, sa, sb = slot_sizes(dims)
    rows = outs[0].shape[0] // sa
    came = []
    for rb in range(1, sb):
        came.append(hop(outs[rb], dims, n_head, 2, -rb))
    part = lambda array, ra: array[ra * rows : (ra + 1) * rows]
    line = []
    for ra in range(1, sa):
        total = add_all(part(outs[0], ra), [part(c, ra) for c in came], jnp.bfloat16)
        line.append(hop(total, dims, n_head, 1, -ra))
    total = add_all(part(outs[0], 0), [part(c, 0) for c in came] + line, jnp.bfloat16)
    if r0 == 0:
        return total
    return hop(total, dims, n_head, 0, -r0)


def slot_source(key, dims):
    place = lax.axis_index("ctx")
    core = lax.axis_index("head") % 2
    orders = phase_dims(dims)
    sources = []
    for order in orders:
        coords = [place // (dims[1] * dims[2]), place // dims[2] % dims[1], place % dims[2]]
        for dim, by in zip(order, key, strict=True):
            coords[dim] = (coords[dim] - by) % dims[dim]
        sources.append((coords[0] * dims[1] + coords[1]) * dims[2] + coords[2])
    return jnp.where(core == 0, sources[0], sources[1]).astype(jnp.int32)


def expert_body(n_a, n_b, n_expert, cap, n_tiles, src_ref, slot_ref, gate_ref, *refs):
    n_blocks = n_a * n_b
    blocks = refs[:n_blocks]
    gate_own, up_own, down_own, gate_oth, up_oth, down_oth = refs[n_blocks : n_blocks + 6]
    outs = refs[n_blocks + 6 : n_blocks + 6 + n_b]
    picked, hidden_of, scaled, select = refs[n_blocks + 6 + n_b :]
    expert = pl.program_id(0)
    tile = pl.program_id(1)
    tokens = blocks[0].shape[0]

    @pl.when((expert == 0) & (tile == 0))
    def _():
        for b in range(n_blocks):
            src = src_ref[b]
            for e in range(n_expert):
                wanted = slot_ref[src, pl.ds(e, 1), :]
                at = lax.broadcasted_iota(jnp.int32, (cap, tokens), 0)
                hit = (at == jnp.broadcast_to(wanted, (cap, tokens))).astype(jnp.float32)
                select[b, pl.ds(e * cap, cap), :] = hit.astype(jnp.bfloat16)
            got = jnp.dot(select[b], blocks[b][...], preferred_element_type=jnp.float32).astype(
                jnp.bfloat16
            )
            for e in range(n_expert):
                picked[e, pl.ds(b * cap, cap), :] = got[e * cap : (e + 1) * cap]

    def step(w_gate, w_up):
        tokens_in = picked[expert]
        gate_h = jnp.dot(tokens_in, w_gate[0], preferred_element_type=jnp.float32)
        up_h = jnp.dot(tokens_in, w_up[0], preferred_element_type=jnp.float32)
        hidden = gate_h * (1.0 / (1.0 + jnp.exp(-gate_h))) * up_h
        hidden_of[tile] = hidden.astype(jnp.bfloat16)

    def finish(w_down):
        hidden = jnp.concatenate([hidden_of[i] for i in range(n_tiles)], axis=1)
        result = jnp.dot(hidden, w_down[0], preferred_element_type=jnp.float32)
        for b in range(n_blocks):
            src = src_ref[b]
            weight_row = gate_ref[src, pl.ds(expert, 1), :]
            hit = select[b, pl.ds(expert * cap, cap), :].astype(jnp.float32)
            weight = jnp.sum(hit * weight_row, axis=1, keepdims=True)
            scaled[b, pl.ds(expert * cap, cap), :] = (
                result[b * cap : (b + 1) * cap] * weight
            ).astype(jnp.bfloat16)

    @pl.when(expert < n_expert // 2)
    def _():
        step(gate_own, up_own)

        @pl.when(tile == n_tiles - 1)
        def _():
            finish(down_own)

    @pl.when(expert >= n_expert // 2)
    def _():
        step(gate_oth, up_oth)

        @pl.when(tile == n_tiles - 1)
        def _():
            finish(down_oth)

    @pl.when((tile == n_tiles - 1) & (expert == n_expert - 1))
    def _():
        for b in range(n_blocks):
            back = jnp.transpose(select[b].astype(jnp.float32)).astype(jnp.bfloat16)
            outs[b // n_a][pl.ds(b % n_a * tokens, tokens), :] = jnp.dot(
                back, scaled[b], preferred_element_type=jnp.float32
            ).astype(jnp.bfloat16)


def run_experts(group, sources, slot_of, gate_of, own, other, cap):
    n_b, n_a = len(group), len(group[0])
    blocks = [block for line in group for block in line]
    n_blocks = len(blocks)
    tokens, width = blocks[0].shape
    per_dev, _, hidden = own[0].shape
    n_expert = 2 * per_dev
    tile_f = 256 if hidden % 256 == 0 else hidden
    n_tiles = hidden // tile_f
    last = n_tiles - 1
    whole = lambda shape: pl.BlockSpec(
        shape, lambda e, f, s: (0,) * len(shape), pipeline_mode=pl.Buffered(1)
    )

    def own_at(e, f):
        here = e < per_dev
        return jnp.where(here, e, per_dev - 1), jnp.where(here, f, last)

    def other_at(e, f):
        here = e >= per_dev
        return jnp.where(here, e - per_dev, 0), jnp.where(here, f, 0)

    def in_spec(at):
        return pl.BlockSpec((1, width, tile_f), lambda e, f, s: (at(e, f)[0], 0, at(e, f)[1]))

    def out_spec(at):
        return pl.BlockSpec((1, hidden, width), lambda e, f, s: (at(e, f)[0], 0, 0))

    rows = n_blocks * cap
    flops = 2 * n_expert * rows * width * hidden * 3
    moved = 2 * (2 * n_blocks * tokens * width + n_expert * 3 * width * hidden)
    return pl.pallas_call(
        functools.partial(expert_body, n_a, n_b, n_expert, cap, n_tiles),
        out_shape=[jax.ShapeDtypeStruct((n_a * tokens, width), jnp.bfloat16)] * n_b,
        grid_spec=pltpu.PrefetchScalarGridSpec(
            num_scalar_prefetch=1,
            grid=(n_expert, n_tiles),
            in_specs=[whole(slot_of.shape), whole(gate_of.shape)]
            + [whole((tokens, width))] * n_blocks
            + [in_spec(own_at), in_spec(own_at), out_spec(own_at)]
            + [in_spec(other_at), in_spec(other_at), out_spec(other_at)],
            out_specs=[whole((n_a * tokens, width))] * n_b,
            scratch_shapes=[
                pltpu.VMEM((n_expert, rows, width), jnp.bfloat16),
                pltpu.VMEM((n_tiles, rows, tile_f), jnp.bfloat16),
                pltpu.VMEM((n_blocks, n_expert * cap, width), jnp.bfloat16),
                pltpu.VMEM((n_blocks, n_expert * cap, tokens), jnp.bfloat16),
            ],
        ),
        compiler_params=pltpu.CompilerParams(
            dimension_semantics=("arbitrary", "arbitrary"), vmem_limit_bytes=60 * 1024 * 1024
        ),
        cost_estimate=pl.CostEstimate(
            flops=flops, bytes_accessed=moved, transcendentals=n_expert * rows * hidden
        ),
    )(sources, slot_of, gate_of, *blocks, *own, *other)


def two_terms(exact):
    high = exact.astype(jnp.bfloat16)
    return high, (exact - high.astype(jnp.float32)).astype(jnp.bfloat16)


def mm(lhs, rhs, at_lhs, at_rhs):
    return lax.dot_general(
        lhs, rhs, (((at_lhs,), (at_rhs,)), ((), ())), preferred_element_type=jnp.float32
    )


def mm_split(exact, narrow, at_lhs, at_rhs):
    high, low = two_terms(exact)
    return mm(high, narrow, at_lhs, at_rhs) + mm(low, narrow, at_lhs, at_rhs)


def unit_rows(vectors):
    floats = vectors.astype(jnp.float32)
    return floats * lax.rsqrt(jnp.sum(floats * floats, axis=-1, keepdims=True) + norm_eps)


def down_rows(row, lanes):
    return jnp.transpose(jnp.broadcast_to(row, (lanes, row.shape[1])))


def prep_body(rows, mine_ref, key_ref, value_ref, cumul_ref, unit_ref, *refs):
    heads, length, depth = key_ref.shape
    plane = heads * depth // rows
    gram_refs, held_refs = refs[:plane], refs[plane : 2 * plane]
    gram_all, held_all = refs[2 * plane :]
    last = cumul_ref[:, length - 1 : length]
    chunk = min(rows, depth)
    for h in range(heads):
        unit = unit_rows(key_ref[h]).astype(jnp.bfloat16)
        unit_ref[h] = unit
        left = last[h : h + 1] - cumul_ref[h : h + 1, :]
        faded = unit.astype(jnp.float32) * jnp.exp(down_rows(left, depth))
        high, low = two_terms(faded)
        gram = mm(high, unit, 0, 0) + mm(low, unit, 0, 0)
        held = mm(value_ref[h], high, 0, 0) + mm(value_ref[h], low, 0, 0)
        for start in range(0, depth, chunk):
            piece, at = divmod(h * depth + start, rows)
            gram_all[piece, at : at + chunk, :] = gram[start : start + chunk]
            held_all[piece, at : at + chunk, :] = held[start : start + chunk]
    tails = jnp.broadcast_to(last, (heads, depth))
    for k in range(plane):
        piece = mine_ref[0] ^ k
        gram_refs[k][0:rows, :] = gram_all[piece]
        gram_refs[k][rows : rows + heads, :] = tails
        held_refs[k][...] = held_all[piece].astype(jnp.bfloat16)


def prep(place, keys, values, cumul_log, plane):
    heads, length, depth = keys.shape
    rows = heads * depth // plane
    outs = (
        [jax.ShapeDtypeStruct(keys.shape, jnp.bfloat16)]
        + [jax.ShapeDtypeStruct((rows + heads, depth), jnp.float32)] * plane
        + [jax.ShapeDtypeStruct((rows, depth), jnp.bfloat16)] * plane
    )
    whole = lambda a: pl.BlockSpec(a.shape, lambda i, s: (0,) * len(a.shape))
    unit, *pieces = pl.pallas_call(
        functools.partial(prep_body, rows),
        out_shape=outs,
        grid_spec=pltpu.PrefetchScalarGridSpec(
            num_scalar_prefetch=1,
            grid=(1,),
            in_specs=[whole(keys), whole(values), whole(cumul_log)],
            out_specs=[whole(out) for out in outs],
            scratch_shapes=[pltpu.VMEM((plane, rows, depth), jnp.float32)] * 2,
        ),
        cost_estimate=pl.CostEstimate(
            flops=8 * heads * length * depth * depth,
            bytes_accessed=8 * heads * length * depth,
            transcendentals=heads * length * depth,
        ),
        name="prep",
    )(place, keys, values, cumul_log)
    return unit, pieces[:plane], pieces[plane:]


def plane_sums(tails, mine):
    count = len(tails)
    upto, before = [], []
    for k in range(count):
        total = jnp.zeros_like(tails[0])
        for j in range(count):
            total = total + jnp.where((mine ^ j) < (mine ^ k), tails[j], 0.0)
        before.append(total)
        upto.append(total + tails[k])
    return upto, before, functools.reduce(lambda x, y: x + y, tails)


def by_row(factors, table_ref, mine, rows, depth):
    table_ref[...] = factors
    span = max(1, rows // depth)
    first = mine * rows // depth
    return [table_ref[pl.ds(first + i, 1), :] for i in range(span)]


def weighted(factors, piece_ref, rows):
    step = rows // len(factors)
    return [
        f * piece_ref[i * step : (i + 1) * step, :].astype(jnp.float32)
        for i, f in enumerate(factors)
    ]


def mid_body(count, rows, tailed, mine_ref, *refs):
    pieces, tail_refs, up_ref, table_ref = refs[:count], refs[count : -2], refs[-2], refs[-1]
    heads, depth = table_ref.shape
    mine = mine_ref[0]
    tails = [t[...] for t in tail_refs]
    upto, _, every = plane_sums(tails, mine)
    total = None
    for k in range(count):
        factors = by_row(jnp.exp(every - upto[k]), table_ref, mine, rows, depth)
        term = weighted(factors, pieces[k], rows)
        total = term if total is None else [x + y for x, y in zip(total, term, strict=True)]
    step = rows // len(total)
    for i, part in enumerate(total):
        up_ref[i * step : (i + 1) * step, :] = part.astype(up_ref.dtype)
    if tailed:
        up_ref[rows : rows + heads, :] = every


def post_body(count, shifts, rows, mine_ref, *refs):
    pieces, tail_refs = refs[:count], refs[count : 2 * count]
    came = refs[2 * count : 2 * count + shifts]
    came_tails = refs[2 * count + shifts : 2 * count + 2 * shifts]
    outs, table_ref = refs[2 * count + 2 * shifts : -1], refs[-1]
    heads, depth = table_ref.shape
    mine = mine_ref[0]
    upto, before, _ = plane_sums([t[...] for t in tail_refs], mine)
    lost = jnp.zeros((heads, depth), jnp.float32)
    below = None
    for r in range(shifts):
        factors = by_row(jnp.exp(lost), table_ref, mine, rows, depth)
        term = weighted(factors, came[r], rows)
        below = term if below is None else [x + y for x, y in zip(below, term, strict=True)]
        lost = lost + came_tails[r][...]
    for k in range(count):
        factors = by_row(jnp.exp(before[k]), table_ref, mine, rows, depth)
        if below is None:
            total = [jnp.zeros((rows // len(factors), depth), jnp.float32)] * len(factors)
        else:
            total = [f * part for f, part in zip(factors, below, strict=True)]
        for j in range(count):
            if j == k:
                continue
            earlier = (mine ^ j) < (mine ^ k)
            share = jnp.where(earlier, jnp.exp(jnp.where(earlier, before[k] - upto[j], 0.0)), 0.0)
            factors = by_row(share, table_ref, mine, rows, depth)
            term = weighted(factors, pieces[j], rows)
            total = [x + y for x, y in zip(total, term, strict=True)]
        step = rows // len(total)
        for i, part in enumerate(total):
            outs[k][i * step : (i + 1) * step, :] = part.astype(outs[k].dtype)


def state_call(body, mine, arrays, blocks, outs, heads, depth):
    fixed = lambda block: pl.BlockSpec(block[0], lambda i, s: block[1])
    return pl.pallas_call(
        body,
        out_shape=outs,
        grid_spec=pltpu.PrefetchScalarGridSpec(
            num_scalar_prefetch=1,
            grid=(1,),
            in_specs=[fixed(block) for block in blocks],
            out_specs=[fixed((out.shape, (0, 0))) for out in outs],
            scratch_shapes=[pltpu.VMEM((heads, depth), jnp.float32)],
        ),
        cost_estimate=pl.CostEstimate(
            flops=2**21, bytes_accessed=2**21, transcendentals=2**12
        ),
    )(mine, *arrays)


def plane_pairs(n_ctx, plane, k):
    return [(i, i // plane * plane + (i % plane ^ k)) for i in range(n_ctx)]


def up_pairs(n_ctx, plane, r):
    return [(i, i + r * plane) for i in range(n_ctx) if i + r * plane < n_ctx]


class Exchange:
    def __init__(self, dims, rows, heads, depth):
        self.dims, self.rows, self.heads, self.depth = dims, rows, heads, depth
        self.plane = dims[1] * dims[2]
        self.n_ctx = dims[0] * self.plane
        self.mine = lax.rem(lax.axis_index("ctx"), self.plane).astype(jnp.int32)
        self.place = self.mine.reshape(1)
        self.whole = ((rows, depth), (0, 0))
        self.tail = ((heads, depth), (rows // heads, 0))

    def send_in(self, pieces):
        got = []
        for k in range(self.plane):
            piece = pieces[k]
            if k:
                piece = lax.ppermute(piece, "ctx", plane_pairs(self.n_ctx, self.plane, k))
            got.append(piece)
        return got

    def totals(self, got, tailed):
        own_tails = got is tailed
        size = self.rows + (self.heads if own_tails else 0)
        out = jax.ShapeDtypeStruct((size, self.depth), got[0].dtype)
        return state_call(
            functools.partial(mid_body, self.plane, self.rows, own_tails),
            self.place,
            [*got, *tailed],
            [self.whole] * self.plane + [self.tail] * self.plane,
            [out],
            self.heads,
            self.depth,
        )[0]

    def send_up(self, up):
        came = []
        for r in range(1, self.dims[0]):
            came.append(lax.ppermute(up, "ctx", up_pairs(self.n_ctx, self.plane, r)))
        return came

    def priors(self, got, tailed, came, came_tailed):
        shifts = self.dims[0] - 1
        out = jax.ShapeDtypeStruct((self.rows, self.depth), got[0].dtype)
        return state_call(
            functools.partial(post_body, self.plane, shifts, self.rows),
            self.place,
            [*got, *tailed, *came, *came_tailed],
            [self.whole] * self.plane
            + [self.tail] * self.plane
            + [self.whole] * shifts
            + [self.tail] * shifts,
            [out] * self.plane,
            self.heads,
            self.depth,
        )

    def send_out(self, priors):
        result = [priors[0]]
        for k in range(1, self.plane):
            result.append(lax.ppermute(priors[k], "ctx", plane_pairs(self.n_ctx, self.plane, k)))
        return result


def causal(cumul):
    length = cumul.shape[1]
    at = lax.broadcasted_iota(jnp.int32, (length, length), 0)
    of = lax.broadcasted_iota(jnp.int32, (length, length), 1)
    gap = down_rows(cumul, length) - jnp.broadcast_to(cumul, (length, length))
    return jnp.where(at >= of, jnp.exp(jnp.where(at >= of, gap, 0.0)), 0.0)


def prior_of(head, piece_refs, mine, depth):
    rows = piece_refs[0].shape[0]
    chunk = min(rows, depth)
    parts = []
    for start in range(0, depth, chunk):
        first = head * depth + start
        piece = first // rows
        at = pl.multiple_of(first % rows, chunk)
        part = jnp.zeros((chunk, depth), jnp.float32)
        for k, ref in enumerate(piece_refs):
            part = jnp.where((piece ^ mine) == k, ref[pl.ds(at, chunk), :].astype(jnp.float32), part)
        parts.append(part)
    return parts[0] if len(parts) == 1 else jnp.concatenate(parts, axis=0)


def solve_body(per_step, mine_ref, query_ref, unit_ref, cumul_ref, ridge_ref, *refs):
    pieces, answer_ref = refs[:-1], refs[-1]
    mine = mine_ref[0]
    length, depth = query_ref.shape[1:]
    spans = range(per_step)
    heads = [pl.program_id(0) * per_step + i for i in spans]
    units = [unit_ref[i] for i in spans]
    shares = [causal(cumul_ref[i]) for i in spans]
    starts = [jnp.exp(down_rows(cumul_ref[i], depth)) for i in spans]
    grams = [two_terms(prior_of(h, pieces, mine, depth)) for h in heads]
    remain = [unit_rows(query_ref[i]) for i in spans]
    direction = list(remain)
    answer = [jnp.zeros((length, depth), jnp.float32) for _ in spans]
    norm_now = [jnp.sum(r * r, axis=-1, keepdims=True) for r in remain]
    for _ in range(CG_STEPS):
        for i in spans:
            high, low = two_terms(direction[i])
            scores = (mm(high, units[i], 1, 1) + mm(low, units[i], 1, 1)) * shares[i]
            g_high, g_low = grams[i]
            prior = mm(high, g_high, 1, 1) + mm(low, g_high, 1, 1) + mm(high, g_low, 1, 1)
            applied = (
                starts[i] * prior
                + mm_split(scores, units[i], 1, 0)
                + ridge_ref[i] * direction[i]
            )
            length_of = norm_now[i] / jnp.sum(direction[i] * applied, axis=-1, keepdims=True)
            answer[i] = answer[i] + length_of * direction[i]
            remain[i] = remain[i] - length_of * applied
            norm_next = jnp.sum(remain[i] * remain[i], axis=-1, keepdims=True)
            direction[i] = remain[i] + (norm_next / norm_now[i]) * direction[i]
            norm_now[i] = norm_next
    for i in spans:
        answer_ref[i] = answer[i]


def read_body(per_step, mine_ref, answer_ref, unit_ref, value_ref, cumul_ref, *refs):
    pieces, out_ref = refs[:-1], refs[-1]
    mine = mine_ref[0]
    depth = answer_ref.shape[2]
    for i in range(per_step):
        head = pl.program_id(0) * per_step + i
        high, low = two_terms(answer_ref[i])
        held = prior_of(head, pieces, mine, depth).astype(jnp.bfloat16)
        start = jnp.exp(down_rows(cumul_ref[i], depth))
        prior = start * (mm(high, held, 1, 1) + mm(low, held, 1, 1))
        scores = (mm(high, unit_ref[i], 1, 1) + mm(low, unit_ref[i], 1, 1)) * causal(cumul_ref[i])
        out = prior + mm_split(scores, value_ref[i], 1, 0)
        out_ref[:, i * depth : (i + 1) * depth] = out.astype(jnp.bfloat16)


def head_call(body, mine, arrays, pieces, out, per_step, flops):
    heads, length, depth = arrays[0].shape
    by_head = lambda a: pl.BlockSpec((per_step, *a.shape[1:]), lambda i, s: (i, 0, 0))
    if len(out.shape) == 3:
        out_spec = by_head(out)
    else:
        out_spec = pl.BlockSpec((length, per_step * depth), lambda i, s: (0, i))
    return pl.pallas_call(
        functools.partial(body, per_step),
        out_shape=out,
        grid_spec=pltpu.PrefetchScalarGridSpec(
            num_scalar_prefetch=1,
            grid=(heads // per_step,),
            in_specs=[by_head(a) for a in arrays]
            + [pl.BlockSpec(p.shape, lambda i, s: (0, 0)) for p in pieces],
            out_specs=out_spec,
        ),
        cost_estimate=pl.CostEstimate(
            flops=flops, bytes_accessed=12 * heads * length * depth, transcendentals=heads * length * length
        ),
    )(mine, *arrays, *pieces)


def on_device(
    queries,
    key_vecs,
    values,
    log_decay,
    ridge_diag,
    residual,
    w_out,
    norm_gain,
    routes,
    gate_probs,
    w_gate,
    w_up,
    w_down,
):
    tok_dev, heads_dev, head_dim = queries.shape
    n_ctx = lax.axis_size("ctx")
    n_head = lax.axis_size("head")
    dims = grid_dims(n_ctx)
    core = lax.axis_index("head")
    swap = [(i, i ^ 1) for i in range(n_head)]

    tok_moe, top_count = routes.shape
    per_dev = w_gate.shape[0]
    expert_total = per_dev * n_ctx * n_head
    cap = 2 * tok_moe * top_count // expert_total
    own = (w_gate, w_up, w_down)
    other = tuple(lax.ppermute(w, "head", swap) for w in own)
    named = routes[:, :, None] == jnp.arange(expert_total, dtype=jnp.int32)[None, None, :]
    dense = jnp.sum(jnp.where(named, gate_probs[:, :, None], 0.0), axis=1)
    table = dense.T.reshape(n_ctx, n_head * per_dev, tok_moe)
    keys_h = key_vecs.transpose(1, 0, 2)
    values_h = values.transpose(1, 0, 2)
    queries_h = queries.transpose(1, 0, 2)
    cumul_log = jnp.cumsum(log_decay, axis=1)
    cumul_h = cumul_log[:, None, :]
    plane = dims[1] * dims[2]
    swap_state = Exchange(dims, heads_dev * head_dim // plane, heads_dev, head_dim)
    unit_h, gram_pieces, held_pieces = prep(swap_state.place, keys_h, values_h, cumul_log, plane)
    gram_got = swap_state.send_in(gram_pieces)
    held_got = swap_state.send_in(held_pieces)
    gram_up = swap_state.totals(gram_got, gram_got)
    gram_came = swap_state.send_up(gram_up)
    held_up = swap_state.totals(held_got, gram_got)
    held_came = swap_state.send_up(held_up)
    gram_prior = swap_state.priors(gram_got, gram_got, gram_came, gram_came)
    gram_prior = swap_state.send_out(gram_prior)
    held_prior = swap_state.priors(held_got, gram_got, held_came, gram_came)
    held_prior = swap_state.send_out(held_prior)
    per_step = 4 if heads_dev % 4 == 0 else 1
    work = heads_dev * tok_dev * head_dim
    answer = head_call(
        solve_body,
        swap_state.place,
        [queries_h, unit_h, cumul_h, ridge_diag[:, None, :]],
        gram_prior,
        jax.ShapeDtypeStruct(queries_h.shape, jnp.float32),
        per_step,
        CG_STEPS * work * (8 * tok_dev + 6 * head_dim),
    )
    mesa_rows = head_call(
        read_body,
        swap_state.place,
        [answer, unit_h, values_h, cumul_h],
        held_prior,
        jax.ShapeDtypeStruct((tok_dev, heads_dev * head_dim), jnp.bfloat16),
        per_step,
        work * (8 * tok_dev + 4 * head_dim),
    )
    partial = jnp.dot(mesa_rows, w_out, preferred_element_type=jnp.float32)
    sent = lax.dynamic_slice_in_dim(partial, (1 - core) * tok_moe, tok_moe, 0)
    came = lax.ppermute(sent.astype(jnp.bfloat16), "head", swap)
    kept = lax.dynamic_slice_in_dim(partial, core * tok_moe, tok_moe, 0)
    attended = (residual.astype(jnp.float32) + kept + came.astype(jnp.float32)).astype(jnp.bfloat16)
    att_f = attended.astype(jnp.float32)
    normed = (
        att_f * lax.rsqrt(jnp.mean(att_f * att_f, axis=-1, keepdims=True) + norm_eps) * norm_gain
    ).astype(jnp.bfloat16)

    groups = spread(normed, dims, n_head)
    gate_of = lax.all_to_all(table, "ctx", split_axis=0, concat_axis=0, tiled=True)
    split = gate_of.reshape(n_ctx, n_head, per_dev, tok_moe)
    gate_of = jnp.where(core == 0, split, split[:, ::-1]).reshape(gate_of.shape)
    routed = (gate_of != 0.0).astype(jnp.bfloat16)
    earlier = (jnp.arange(tok_moe)[:, None] < jnp.arange(tok_moe)[None, :]).astype(jnp.bfloat16)
    before = jnp.einsum("set,tu->seu", routed, earlier, preferred_element_type=jnp.float32)
    slot_of = jnp.where(gate_of != 0.0, before.astype(jnp.int32), -1)

    back = []
    for r0, group in groups.items():
        sources = [
            slot_source((r0, ra, rb), dims) for rb in range(len(group)) for ra in range(len(group[0]))
        ]
        sources = lax.optimization_barrier(jnp.stack(sources))
        outs = run_experts(group, sources, slot_of, gate_of, own, other, cap)
        back.append(collect(outs, r0, dims, n_head))
    layer_out = add_all(att_f, back, jnp.bfloat16)
    return (attended, layer_out)


def solution(mesh):
    in_specs = (
        P("ctx", "head", None),
        P("ctx", "head", None),
        P("ctx", "head", None),
        P("head", "ctx"),
        P("head", None),
        P(("ctx", "head"), None),
        P("head", None),
        P(),
        P(("ctx", "head"), None),
        P(("ctx", "head"), None),
        P(("ctx", "head"), None, None),
        P(("ctx", "head"), None, None),
        P(("ctx", "head"), None, None),
    )
    out_specs = (P(("ctx", "head"), None), P(("ctx", "head"), None))

    return jax.shard_map(
        on_device, mesh=mesh, in_specs=in_specs, out_specs=out_specs, check_vma=False
    )
```

```python
import functools

import jax
import jax.numpy as jnp
from jax import lax
from jax.experimental import pallas as pl
from jax.experimental.pallas import tpu as pltpu
from jax.sharding import PartitionSpec as P

CG_STEPS = 4

norm_eps = 1e-06
BOTH = ("ctx", "head")


def grid_dims(count):
    bits = count.bit_length() - 1
    if 1 << bits != count:
        return (count, 1, 1)
    first = -(-bits // 3)
    second = -(-(bits - first) // 2)
    return (1 << first, 1 << second, 1 << (bits - first - second))


def shifted(place, dims, dim, by):
    coords = [place // (dims[1] * dims[2]), place // dims[2] % dims[1], place % dims[2]]
    coords[dim] = (coords[dim] + by) % dims[dim]
    return (coords[0] * dims[1] + coords[1]) * dims[2] + coords[2]


def phase_dims(dims):
    if dims[1] == dims[2]:
        return ((0, 2, 1), (0, 1, 2))
    return ((0, 2, 1), (0, 2, 1))


def hop(block, dims, n_head, phase, by):
    orders = phase_dims(dims)
    count = dims[0] * dims[1] * dims[2]
    pairs = []
    for place in range(count):
        for core in range(n_head):
            dest = shifted(place, dims, orders[core % 2][phase], by)
            pairs.append((place * n_head + core, dest * n_head + core))
    return lax.ppermute(block, BOTH, pairs)


def slot_sizes(dims):
    order = phase_dims(dims)[0]
    return tuple(dims[d] for d in order)


def spread(block, dims, n_head):
    s0, sa, sb = slot_sizes(dims)
    heads = {0: block}
    for r0 in range(1, s0):
        heads[r0] = hop(block, dims, n_head, 0, r0)
    groups = {}
    for r0 in visit(s0):
        head = heads[r0]
        line = [head]
        for ra in range(1, sa):
            line.append(hop(head, dims, n_head, 1, ra))
        group = [line]
        for rb in range(1, sb):
            sent = [hop(head, dims, n_head, 2, rb)]
            sent += [hop(one, dims, n_head, 2, rb) for one in line[1:]]
            group.append(sent)
        groups[r0] = group
    return groups


def visit(size):
    return [*range(1, size), 0]


def add_all(first, others, dtype):
    total = first.astype(jnp.float32)
    for other in others:
        total = total + other.astype(jnp.float32)
    return total.astype(dtype)


def collect(outs, r0, dims, n_head):
    _, sa, sb = slot_sizes(dims)
    rows = outs[0].shape[0] // sa
    came = []
    for rb in range(1, sb):
        came.append(hop(outs[rb], dims, n_head, 2, -rb))
    part = lambda array, ra: array[ra * rows : (ra + 1) * rows]
    line = []
    for ra in range(1, sa):
        total = add_all(part(outs[0], ra), [part(c, ra) for c in came], jnp.bfloat16)
        line.append(hop(total, dims, n_head, 1, -ra))
    total = add_all(part(outs[0], 0), [part(c, 0) for c in came] + line, jnp.bfloat16)
    if r0 == 0:
        return total
    return hop(total, dims, n_head, 0, -r0)


def slot_source(key, dims):
    place = lax.axis_index("ctx")
    core = lax.axis_index("head") % 2
    orders = phase_dims(dims)
    sources = []
    for order in orders:
        coords = [place // (dims[1] * dims[2]), place // dims[2] % dims[1], place % dims[2]]
        for dim, by in zip(order, key, strict=True):
            coords[dim] = (coords[dim] - by) % dims[dim]
        sources.append((coords[0] * dims[1] + coords[1]) * dims[2] + coords[2])
    return jnp.where(core == 0, sources[0], sources[1]).astype(jnp.int32)


def expert_body(n_a, n_b, n_expert, cap, n_tiles, src_ref, slot_ref, gate_ref, *refs):
    n_blocks = n_a * n_b
    blocks = refs[:n_blocks]
    gate_own, up_own, down_own, gate_oth, up_oth, down_oth = refs[n_blocks : n_blocks + 6]
    outs = refs[n_blocks + 6 : n_blocks + 6 + n_b]
    picked, hidden_of, scaled, select = refs[n_blocks + 6 + n_b :]
    expert = pl.program_id(0)
    tile = pl.program_id(1)
    tokens = blocks[0].shape[0]

    @pl.when((expert == 0) & (tile == 0))
    def _():
        for b in range(n_blocks):
            src = src_ref[b]
            for e in range(n_expert):
                wanted = slot_ref[src, pl.ds(e, 1), :]
                at = lax.broadcasted_iota(jnp.int32, (cap, tokens), 0)
                hit = (at == jnp.broadcast_to(wanted, (cap, tokens))).astype(jnp.float32)
                select[b, pl.ds(e * cap, cap), :] = hit.astype(jnp.bfloat16)
            got = jnp.dot(select[b], blocks[b][...], preferred_element_type=jnp.float32).astype(
                jnp.bfloat16
            )
            for e in range(n_expert):
                picked[e, pl.ds(b * cap, cap), :] = got[e * cap : (e + 1) * cap]

    def step(w_gate, w_up):
        tokens_in = picked[expert]
        gate_h = jnp.dot(tokens_in, w_gate[0], preferred_element_type=jnp.float32)
        up_h = jnp.dot(tokens_in, w_up[0], preferred_element_type=jnp.float32)
        hidden = gate_h * (1.0 / (1.0 + jnp.exp(-gate_h))) * up_h
        hidden_of[tile] = hidden.astype(jnp.bfloat16)

    def finish(w_down):
        hidden = jnp.concatenate([hidden_of[i] for i in range(n_tiles)], axis=1)
        result = jnp.dot(hidden, w_down[0], preferred_element_type=jnp.float32)
        for b in range(n_blocks):
            src = src_ref[b]
            weight_row = gate_ref[src, pl.ds(expert, 1), :]
            hit = select[b, pl.ds(expert * cap, cap), :].astype(jnp.float32)
            weight = jnp.sum(hit * weight_row, axis=1, keepdims=True)
            scaled[b, pl.ds(expert * cap, cap), :] = (
                result[b * cap : (b + 1) * cap] * weight
            ).astype(jnp.bfloat16)

    @pl.when(expert < n_expert // 2)
    def _():
        step(gate_own, up_own)

        @pl.when(tile == n_tiles - 1)
        def _():
            finish(down_own)

    @pl.when(expert >= n_expert // 2)
    def _():
        step(gate_oth, up_oth)

        @pl.when(tile == n_tiles - 1)
        def _():
            finish(down_oth)

    @pl.when((tile == n_tiles - 1) & (expert == n_expert - 1))
    def _():
        for b in range(n_blocks):
            back = jnp.transpose(select[b].astype(jnp.float32)).astype(jnp.bfloat16)
            outs[b // n_a][pl.ds(b % n_a * tokens, tokens), :] = jnp.dot(
                back, scaled[b], preferred_element_type=jnp.float32
            ).astype(jnp.bfloat16)


def run_experts(group, sources, slot_of, gate_of, own, other, cap):
    n_b, n_a = len(group), len(group[0])
    blocks = [block for line in group for block in line]
    n_blocks = len(blocks)
    tokens, width = blocks[0].shape
    per_dev, _, hidden = own[0].shape
    n_expert = 2 * per_dev
    tile_f = 256 if hidden % 256 == 0 else hidden
    n_tiles = hidden // tile_f
    last = n_tiles - 1
    whole = lambda shape: pl.BlockSpec(
        shape, lambda e, f, s: (0,) * len(shape), pipeline_mode=pl.Buffered(1)
    )

    def own_at(e, f):
        here = e < per_dev
        return jnp.where(here, e, per_dev - 1), jnp.where(here, f, last)

    def other_at(e, f):
        here = e >= per_dev
        return jnp.where(here, e - per_dev, 0), jnp.where(here, f, 0)

    def in_spec(at):
        return pl.BlockSpec((1, width, tile_f), lambda e, f, s: (at(e, f)[0], 0, at(e, f)[1]))

    def out_spec(at):
        return pl.BlockSpec((1, hidden, width), lambda e, f, s: (at(e, f)[0], 0, 0))

    rows = n_blocks * cap
    flops = 2 * n_expert * rows * width * hidden * 3
    moved = 2 * (2 * n_blocks * tokens * width + n_expert * 3 * width * hidden)
    return pl.pallas_call(
        functools.partial(expert_body, n_a, n_b, n_expert, cap, n_tiles),
        out_shape=[jax.ShapeDtypeStruct((n_a * tokens, width), jnp.bfloat16)] * n_b,
        grid_spec=pltpu.PrefetchScalarGridSpec(
            num_scalar_prefetch=1,
            grid=(n_expert, n_tiles),
            in_specs=[whole(slot_of.shape), whole(gate_of.shape)]
            + [whole((tokens, width))] * n_blocks
            + [in_spec(own_at), in_spec(own_at), out_spec(own_at)]
            + [in_spec(other_at), in_spec(other_at), out_spec(other_at)],
            out_specs=[whole((n_a * tokens, width))] * n_b,
            scratch_shapes=[
                pltpu.VMEM((n_expert, rows, width), jnp.bfloat16),
                pltpu.VMEM((n_tiles, rows, tile_f), jnp.bfloat16),
                pltpu.VMEM((n_blocks, n_expert * cap, width), jnp.bfloat16),
                pltpu.VMEM((n_blocks, n_expert * cap, tokens), jnp.bfloat16),
            ],
        ),
        compiler_params=pltpu.CompilerParams(
            dimension_semantics=("arbitrary", "arbitrary"), vmem_limit_bytes=60 * 1024 * 1024
        ),
        cost_estimate=pl.CostEstimate(
            flops=flops, bytes_accessed=moved, transcendentals=n_expert * rows * hidden
        ),
    )(sources, slot_of, gate_of, *blocks, *own, *other)


def two_terms(exact):
    high = exact.astype(jnp.bfloat16)
    return high, (exact - high.astype(jnp.float32)).astype(jnp.bfloat16)


def mm(lhs, rhs, at_lhs, at_rhs):
    return lax.dot_general(
        lhs, rhs, (((at_lhs,), (at_rhs,)), ((), ())), preferred_element_type=jnp.float32
    )


def mm_split(exact, narrow, at_lhs, at_rhs):
    high, low = two_terms(exact)
    return mm(high, narrow, at_lhs, at_rhs) + mm(low, narrow, at_lhs, at_rhs)


def unit_rows(vectors):
    floats = vectors.astype(jnp.float32)
    return floats * lax.rsqrt(jnp.sum(floats * floats, axis=-1, keepdims=True) + norm_eps)


def down_rows(row, lanes):
    return jnp.transpose(jnp.broadcast_to(row, (lanes, row.shape[1])))


def prep_body(rows, mine_ref, key_ref, value_ref, cumul_ref, unit_ref, *refs):
    heads, length, depth = key_ref.shape
    plane = heads * depth // rows
    gram_refs, held_refs = refs[:plane], refs[plane : 2 * plane]
    gram_all, held_all = refs[2 * plane :]
    last = cumul_ref[:, length - 1 : length]
    chunk = min(rows, depth)
    for h in range(heads):
        unit = unit_rows(key_ref[h]).astype(jnp.bfloat16)
        unit_ref[h] = unit
        left = last[h : h + 1] - cumul_ref[h : h + 1, :]
        faded = unit.astype(jnp.float32) * jnp.exp(down_rows(left, depth))
        high, low = two_terms(faded)
        gram = mm(high, unit, 0, 0) + mm(low, unit, 0, 0)
        held = mm(value_ref[h], high, 0, 0) + mm(value_ref[h], low, 0, 0)
        for start in range(0, depth, chunk):
            piece, at = divmod(h * depth + start, rows)
            gram_all[piece, at : at + chunk, :] = gram[start : start + chunk]
            held_all[piece, at : at + chunk, :] = held[start : start + chunk]
    tails = jnp.broadcast_to(last, (heads, depth))
    for k in range(plane):
        piece = mine_ref[0] ^ k
        gram_refs[k][0:rows, :] = gram_all[piece]
        gram_refs[k][rows : rows + heads, :] = tails
        held_refs[k][...] = held_all[piece].astype(jnp.bfloat16)


def prep(place, keys, values, cumul_log, plane):
    heads, length, depth = keys.shape
    rows = heads * depth // plane
    outs = (
        [jax.ShapeDtypeStruct(keys.shape, jnp.bfloat16)]
        + [jax.ShapeDtypeStruct((rows + heads, depth), jnp.float32)] * plane
        + [jax.ShapeDtypeStruct((rows, depth), jnp.bfloat16)] * plane
    )
    whole = lambda a: pl.BlockSpec(a.shape, lambda i, s: (0,) * len(a.shape))
    unit, *pieces = pl.pallas_call(
        functools.partial(prep_body, rows),
        out_shape=outs,
        grid_spec=pltpu.PrefetchScalarGridSpec(
            num_scalar_prefetch=1,
            grid=(1,),
            in_specs=[whole(keys), whole(values), whole(cumul_log)],
            out_specs=[whole(out) for out in outs],
            scratch_shapes=[pltpu.VMEM((plane, rows, depth), jnp.float32)] * 2,
        ),
        cost_estimate=pl.CostEstimate(
            flops=8 * heads * length * depth * depth,
            bytes_accessed=8 * heads * length * depth,
            transcendentals=heads * length * depth,
        ),
        name="prep",
    )(place, keys, values, cumul_log)
    return unit, pieces[:plane], pieces[plane:]


def plane_sums(tails, mine):
    count = len(tails)
    upto, before = [], []
    for k in range(count):
        total = jnp.zeros_like(tails[0])
        for j in range(count):
            total = total + jnp.where((mine ^ j) < (mine ^ k), tails[j], 0.0)
        before.append(total)
        upto.append(total + tails[k])
    return upto, before, functools.reduce(lambda x, y: x + y, tails)


def by_row(factors, table_ref, mine, rows, depth):
    table_ref[...] = factors
    span = max(1, rows // depth)
    first = mine * rows // depth
    return [table_ref[pl.ds(first + i, 1), :] for i in range(span)]


def weighted(factors, piece_ref, rows):
    step = rows // len(factors)
    return [
        f * piece_ref[i * step : (i + 1) * step, :].astype(jnp.float32)
        for i, f in enumerate(factors)
    ]


def mid_body(count, rows, tailed, mine_ref, *refs):
    pieces, tail_refs, up_ref, table_ref = refs[:count], refs[count : -2], refs[-2], refs[-1]
    heads, depth = table_ref.shape
    mine = mine_ref[0]
    tails = [t[...] for t in tail_refs]
    upto, _, every = plane_sums(tails, mine)
    total = None
    for k in range(count):
        factors = by_row(jnp.exp(every - upto[k]), table_ref, mine, rows, depth)
        term = weighted(factors, pieces[k], rows)
        total = term if total is None else [x + y for x, y in zip(total, term, strict=True)]
    step = rows // len(total)
    for i, part in enumerate(total):
        up_ref[i * step : (i + 1) * step, :] = part.astype(up_ref.dtype)
    if tailed:
        up_ref[rows : rows + heads, :] = every


def post_body(count, shifts, rows, mine_ref, *refs):
    pieces, tail_refs = refs[:count], refs[count : 2 * count]
    came = refs[2 * count : 2 * count + shifts]
    came_tails = refs[2 * count + shifts : 2 * count + 2 * shifts]
    outs, table_ref = refs[2 * count + 2 * shifts : -1], refs[-1]
    heads, depth = table_ref.shape
    mine = mine_ref[0]
    upto, before, _ = plane_sums([t[...] for t in tail_refs], mine)
    lost = jnp.zeros((heads, depth), jnp.float32)
    below = None
    for r in range(shifts):
        factors = by_row(jnp.exp(lost), table_ref, mine, rows, depth)
        term = weighted(factors, came[r], rows)
        below = term if below is None else [x + y for x, y in zip(below, term, strict=True)]
        lost = lost + came_tails[r][...]
    for k in range(count):
        factors = by_row(jnp.exp(before[k]), table_ref, mine, rows, depth)
        if below is None:
            total = [jnp.zeros((rows // len(factors), depth), jnp.float32)] * len(factors)
        else:
            total = [f * part for f, part in zip(factors, below, strict=True)]
        for j in range(count):
            if j == k:
                continue
            earlier = (mine ^ j) < (mine ^ k)
            share = jnp.where(earlier, jnp.exp(jnp.where(earlier, before[k] - upto[j], 0.0)), 0.0)
            factors = by_row(share, table_ref, mine, rows, depth)
            term = weighted(factors, pieces[j], rows)
            total = [x + y for x, y in zip(total, term, strict=True)]
        step = rows // len(total)
        for i, part in enumerate(total):
            outs[k][i * step : (i + 1) * step, :] = part.astype(outs[k].dtype)


def state_call(body, mine, arrays, blocks, outs, heads, depth):
    fixed = lambda block: pl.BlockSpec(block[0], lambda i, s: block[1])
    return pl.pallas_call(
        body,
        out_shape=outs,
        grid_spec=pltpu.PrefetchScalarGridSpec(
            num_scalar_prefetch=1,
            grid=(1,),
            in_specs=[fixed(block) for block in blocks],
            out_specs=[fixed((out.shape, (0, 0))) for out in outs],
            scratch_shapes=[pltpu.VMEM((heads, depth), jnp.float32)],
        ),
        cost_estimate=pl.CostEstimate(
            flops=2**21, bytes_accessed=2**21, transcendentals=2**12
        ),
    )(mine, *arrays)


def plane_pairs(n_ctx, plane, k):
    return [(i, i // plane * plane + (i % plane ^ k)) for i in range(n_ctx)]


def up_pairs(n_ctx, plane, r):
    return [(i, i + r * plane) for i in range(n_ctx) if i + r * plane < n_ctx]


class Exchange:
    def __init__(self, dims, rows, heads, depth):
        self.dims, self.rows, self.heads, self.depth = dims, rows, heads, depth
        self.plane = dims[1] * dims[2]
        self.n_ctx = dims[0] * self.plane
        self.mine = lax.rem(lax.axis_index("ctx"), self.plane).astype(jnp.int32)
        self.place = self.mine.reshape(1)
        self.whole = ((rows, depth), (0, 0))
        self.tail = ((heads, depth), (rows // heads, 0))

    def send_in(self, pieces):
        got = []
        for k in range(self.plane):
            piece = pieces[k]
            if k:
                piece = lax.ppermute(piece, "ctx", plane_pairs(self.n_ctx, self.plane, k))
            got.append(piece)
        return got

    def totals(self, got, tailed):
        own_tails = got is tailed
        size = self.rows + (self.heads if own_tails else 0)
        out = jax.ShapeDtypeStruct((size, self.depth), got[0].dtype)
        return state_call(
            functools.partial(mid_body, self.plane, self.rows, own_tails),
            self.place,
            [*got, *tailed],
            [self.whole] * self.plane + [self.tail] * self.plane,
            [out],
            self.heads,
            self.depth,
        )[0]

    def send_up(self, up):
        came = []
        for r in range(1, self.dims[0]):
            came.append(lax.ppermute(up, "ctx", up_pairs(self.n_ctx, self.plane, r)))
        return came

    def priors(self, got, tailed, came, came_tailed):
        shifts = self.dims[0] - 1
        out = jax.ShapeDtypeStruct((self.rows, self.depth), got[0].dtype)
        return state_call(
            functools.partial(post_body, self.plane, shifts, self.rows),
            self.place,
            [*got, *tailed, *came, *came_tailed],
            [self.whole] * self.plane
            + [self.tail] * self.plane
            + [self.whole] * shifts
            + [self.tail] * shifts,
            [out] * self.plane,
            self.heads,
            self.depth,
        )

    def send_out(self, priors):
        result = [priors[0]]
        for k in range(1, self.plane):
            result.append(lax.ppermute(priors[k], "ctx", plane_pairs(self.n_ctx, self.plane, k)))
        return result


def causal(cumul):
    length = cumul.shape[1]
    at = lax.broadcasted_iota(jnp.int32, (length, length), 0)
    of = lax.broadcasted_iota(jnp.int32, (length, length), 1)
    gap = down_rows(cumul, length) - jnp.broadcast_to(cumul, (length, length))
    return jnp.where(at >= of, jnp.exp(jnp.where(at >= of, gap, 0.0)), 0.0)


def prior_of(head, piece_refs, mine, depth):
    rows = piece_refs[0].shape[0]
    chunk = min(rows, depth)
    parts = []
    for start in range(0, depth, chunk):
        first = head * depth + start
        piece = first // rows
        at = pl.multiple_of(first % rows, chunk)
        part = jnp.zeros((chunk, depth), jnp.float32)
        for k, ref in enumerate(piece_refs):
            part = jnp.where((piece ^ mine) == k, ref[pl.ds(at, chunk), :].astype(jnp.float32), part)
        parts.append(part)
    return parts[0] if len(parts) == 1 else jnp.concatenate(parts, axis=0)


def solve_body(per_step, mine_ref, query_ref, unit_ref, cumul_ref, ridge_ref, *refs):
    pieces, answer_ref = refs[:-1], refs[-1]
    mine = mine_ref[0]
    length, depth = query_ref.shape[1:]
    spans = range(per_step)
    heads = [pl.program_id(0) * per_step + i for i in spans]
    units = [unit_ref[i] for i in spans]
    shares = [causal(cumul_ref[i]) for i in spans]
    starts = [jnp.exp(down_rows(cumul_ref[i], depth)) for i in spans]
    grams = [two_terms(prior_of(h, pieces, mine, depth)) for h in heads]
    remain = [unit_rows(query_ref[i]) for i in spans]
    direction = list(remain)
    answer = [jnp.zeros((length, depth), jnp.float32) for _ in spans]
    norm_now = [jnp.sum(r * r, axis=-1, keepdims=True) for r in remain]
    for _ in range(CG_STEPS):
        for i in spans:
            high, low = two_terms(direction[i])
            scores = (mm(high, units[i], 1, 1) + mm(low, units[i], 1, 1)) * shares[i]
            g_high, g_low = grams[i]
            prior = mm(high, g_high, 1, 1) + mm(low, g_high, 1, 1) + mm(high, g_low, 1, 1)
            applied = (
                starts[i] * prior
                + mm_split(scores, units[i], 1, 0)
                + ridge_ref[i] * direction[i]
            )
            length_of = norm_now[i] / jnp.sum(direction[i] * applied, axis=-1, keepdims=True)
            answer[i] = answer[i] + length_of * direction[i]
            remain[i] = remain[i] - length_of * applied
            norm_next = jnp.sum(remain[i] * remain[i], axis=-1, keepdims=True)
            direction[i] = remain[i] + (norm_next / norm_now[i]) * direction[i]
            norm_now[i] = norm_next
    for i in spans:
        answer_ref[i] = answer[i]


def read_body(per_step, mine_ref, answer_ref, unit_ref, value_ref, cumul_ref, *refs):
    pieces, out_ref = refs[:-1], refs[-1]
    mine = mine_ref[0]
    depth = answer_ref.shape[2]
    for i in range(per_step):
        head = pl.program_id(0) * per_step + i
        high, low = two_terms(answer_ref[i])
        held = prior_of(head, pieces, mine, depth).astype(jnp.bfloat16)
        start = jnp.exp(down_rows(cumul_ref[i], depth))
        prior = start * (mm(high, held, 1, 1) + mm(low, held, 1, 1))
        scores = (mm(high, unit_ref[i], 1, 1) + mm(low, unit_ref[i], 1, 1)) * causal(cumul_ref[i])
        out = prior + mm_split(scores, value_ref[i], 1, 0)
        out_ref[:, i * depth : (i + 1) * depth] = out.astype(jnp.bfloat16)


def head_call(body, mine, arrays, pieces, out, per_step, flops):
    heads, length, depth = arrays[0].shape
    by_head = lambda a: pl.BlockSpec((per_step, *a.shape[1:]), lambda i, s: (i, 0, 0))
    if len(out.shape) == 3:
        out_spec = by_head(out)
    else:
        out_spec = pl.BlockSpec((length, per_step * depth), lambda i, s: (0, i))
    return pl.pallas_call(
        functools.partial(body, per_step),
        out_shape=out,
        grid_spec=pltpu.PrefetchScalarGridSpec(
            num_scalar_prefetch=1,
            grid=(heads // per_step,),
            in_specs=[by_head(a) for a in arrays]
            + [pl.BlockSpec(p.shape, lambda i, s: (0, 0)) for p in pieces],
            out_specs=out_spec,
        ),
        cost_estimate=pl.CostEstimate(
            flops=flops, bytes_accessed=12 * heads * length * depth, transcendentals=heads * length * length
        ),
    )(mine, *arrays, *pieces)


def on_device(
    queries,
    key_vecs,
    values,
    log_decay,
    ridge_diag,
    residual,
    w_out,
    norm_gain,
    routes,
    gate_probs,
    w_gate,
    w_up,
    w_down,
):
    tok_dev, heads_dev, head_dim = queries.shape
    n_ctx = lax.axis_size("ctx")
    n_head = lax.axis_size("head")
    dims = grid_dims(n_ctx)
    core = lax.axis_index("head")
    swap = [(i, i ^ 1) for i in range(n_head)]

    tok_moe, top_count = routes.shape
    per_dev = w_gate.shape[0]
    expert_total = per_dev * n_ctx * n_head
    cap = 2 * tok_moe * top_count // expert_total
    own = (w_gate, w_up, w_down)
    other = tuple(lax.ppermute(w, "head", swap) for w in own)
    named = routes[:, :, None] == jnp.arange(expert_total, dtype=jnp.int32)[None, None, :]
    dense = jnp.sum(jnp.where(named, gate_probs[:, :, None], 0.0), axis=1)
    table = dense.T.reshape(n_ctx, n_head * per_dev, tok_moe)
    keys_h = key_vecs.transpose(1, 0, 2)
    values_h = values.transpose(1, 0, 2)
    queries_h = queries.transpose(1, 0, 2)
    cumul_log = jnp.cumsum(log_decay, axis=1)
    cumul_h = cumul_log[:, None, :]
    plane = dims[1] * dims[2]
    swap_state = Exchange(dims, heads_dev * head_dim // plane, heads_dev, head_dim)
    unit_h, gram_pieces, held_pieces = prep(swap_state.place, keys_h, values_h, cumul_log, plane)
    gram_got = swap_state.send_in(gram_pieces)
    held_got = swap_state.send_in(held_pieces)
    gram_up = swap_state.totals(gram_got, gram_got)
    gram_came = swap_state.send_up(gram_up)
    held_up = swap_state.totals(held_got, gram_got)
    held_came = swap_state.send_up(held_up)
    gram_prior = swap_state.priors(gram_got, gram_got, gram_came, gram_came)
    gram_prior = swap_state.send_out(gram_prior)
    held_prior = swap_state.priors(held_got, gram_got, held_came, gram_came)
    held_prior = swap_state.send_out(held_prior)
    per_step = 4 if heads_dev % 4 == 0 else 1
    work = heads_dev * tok_dev * head_dim
    answer = head_call(
        solve_body,
        swap_state.place,
        [queries_h, unit_h, cumul_h, ridge_diag[:, None, :]],
        gram_prior,
        jax.ShapeDtypeStruct(queries_h.shape, jnp.float32),
        per_step,
        CG_STEPS * work * (8 * tok_dev + 6 * head_dim),
    )
    mesa_rows = head_call(
        read_body,
        swap_state.place,
        [answer, unit_h, values_h, cumul_h],
        held_prior,
        jax.ShapeDtypeStruct((tok_dev, heads_dev * head_dim), jnp.bfloat16),
        per_step,
        work * (8 * tok_dev + 4 * head_dim),
    )
    partial = jnp.dot(mesa_rows, w_out, preferred_element_type=jnp.float32)
    sent = lax.dynamic_slice_in_dim(partial, (1 - core) * tok_moe, tok_moe, 0)
    came = lax.ppermute(sent.astype(jnp.bfloat16), "head", swap)
    kept = lax.dynamic_slice_in_dim(partial, core * tok_moe, tok_moe, 0)
    attended = (residual.astype(jnp.float32) + kept + came.astype(jnp.float32)).astype(jnp.bfloat16)
    att_f = attended.astype(jnp.float32)
    normed = (
        att_f * lax.rsqrt(jnp.mean(att_f * att_f, axis=-1, keepdims=True) + norm_eps) * norm_gain
    ).astype(jnp.bfloat16)

    groups = spread(normed, dims, n_head)
    gate_of = lax.all_to_all(table, "ctx", split_axis=0, concat_axis=0, tiled=True)
    split = gate_of.reshape(n_ctx, n_head, per_dev, tok_moe)
    gate_of = jnp.where(core == 0, split, split[:, ::-1]).reshape(gate_of.shape)
    routed = (gate_of != 0.0).astype(jnp.bfloat16)
    earlier = (jnp.arange(tok_moe)[:, None] < jnp.arange(tok_moe)[None, :]).astype(jnp.bfloat16)
    before = jnp.einsum("set,tu->seu", routed, earlier, preferred_element_type=jnp.float32)
    slot_of = jnp.where(gate_of != 0.0, before.astype(jnp.int32), -1)

    back = []
    for r0, group in groups.items():
        sources = [
            slot_source((r0, ra, rb), dims) for rb in range(len(group)) for ra in range(len(group[0]))
        ]
        sources = lax.optimization_barrier(jnp.stack(sources))
        outs = run_experts(group, sources, slot_of, gate_of, own, other, cap)
        back.append(collect(outs, r0, dims, n_head))
    layer_out = add_all(att_f, back, jnp.bfloat16)
    return (attended, layer_out)


def solution(mesh):
    in_specs = (
        P("ctx", "head", None),
        P("ctx", "head", None),
        P("ctx", "head", None),
        P("head", "ctx"),
        P("head", None),
        P(("ctx", "head"), None),
        P("head", None),
        P(),
        P(("ctx", "head"), None),
        P(("ctx", "head"), None),
        P(("ctx", "head"), None, None),
        P(("ctx", "head"), None, None),
        P(("ctx", "head"), None, None),
    )
    out_specs = (P(("ctx", "head"), None), P(("ctx", "head"), None))

    return jax.shard_map(
        on_device, mesh=mesh, in_specs=in_specs, out_specs=out_specs, check_vma=False
    )
```
